128 devices in a mesh: grp: 8 (over x, core), tp: 16 (over z, y).
Axes of the slice: x: 4, y: 4, z: 4, core: 2. Of those that a mesh axis runs over, the one named last changes fastest.
Arguments:
- hidden_states: bfloat16 [2048, 8192], P('grp', 'tp'), may hold values from -6 to 6
- norm_gain: float32 [8192], replicated, may hold values from 0.5 to 1.5
- w_query: bfloat16 [8192, 8192], P(None, 'tp'), may hold values from -0.0625 to 0.0625
- w_key: bfloat16 [8192, 1024], P(None, 'tp'), may hold values from -0.0625 to 0.0625
- w_value: bfloat16 [8192, 1024], P(None, 'tp'), may hold values from -0.0625 to 0.0625
- cache: bfloat16 [16384, 2048], P('grp', 'tp'), may hold values from -82 to 82
- w_out: bfloat16 [8192, 8192], P('tp'), may hold values from -6 to 6
Outputs:
- mixed: bfloat16 [2048, 8192], P('grp', 'tp')
The draws below stay inside these ranges and needn't reach their ends.
All inputs are finite; a program needn't handle non-finite values.
Results may differ from the reference program's by a relative error of at most 0.03.
Values may be sent and summed in bfloat16 or wider, within the bound.
A program may use at most 128 MiB of HBM per device.

```python
import math
import jax
import jax.numpy as jnp
from jax import lax

D = 8192
HEADS = 64
KV_HEADS = 8
HEAD_DIM = 128
ROWS = 256
PREFIX = 16384
TOKENS = 2048


def draw_cache(key, part):
    columns = 2 * KV_HEADS * HEAD_DIM
    base = jax.random.normal(key, (PREFIX, columns), jnp.float32)
    return base.astype(jnp.bfloat16)


def levels(rng, shape, pieces, smallest, largest):
    level = 1.0
    for dim, parts in pieces:
        steps = jax.random.uniform(jax.random.fold_in(jax.random.fold_in(rng, 6), dim), (parts,), jnp.float32, smallest / len(pieces), largest / len(pieces))
        level = level * jnp.repeat(jnp.exp(steps), shape[dim] // parts).reshape((-1,) + (1,) * (len(shape) - 1 - dim))
    return level


def gaussian(own_key, dims, width, most, cuts=(), kind=jnp.bfloat16):
    factor_of = levels(own_key, dims, cuts, -0.22, 0.18) if cuts else 1.0
    result = jax.random.normal(own_key, dims, jnp.float32) * width * factor_of
    return jnp.minimum(jnp.maximum(result, -most), most).astype(kind)


def setup_inputs(seed: int = 0) -> dict:
    key_of = jax.random.split(jax.random.key(seed), 8)
    hidden_states = gaussian(key_of[0], (TOKENS, D), 1.0, 6.0, ((0, 8), (1, 16)))
    norm_gain = jnp.clip(1.0 + 0.1 * jax.random.normal(key_of[1], (D,), jnp.float32), 0.5, 1.5)
    w_query = gaussian(key_of[2], (D, HEADS * HEAD_DIM), D ** -0.5, 0.0625, ((1, 16),))
    w_key = gaussian(key_of[3], (D, KV_HEADS * HEAD_DIM), D ** -0.5, 0.0625, ((1, 16),))
    w_value = gaussian(key_of[4], (D, KV_HEADS * HEAD_DIM), D ** -0.5, 0.0625, ((1, 16),))
    cache = draw_cache(jax.random.fold_in(key_of[7], 71), 0)
    w_out = gaussian(key_of[6], (HEADS * HEAD_DIM, D), 1.0, 6.0, ((0, 16),))
    return {"hidden_states": hidden_states, "norm_gain": norm_gain, "w_query": w_query, "w_key": w_key, "w_value": w_value, "cache": cache, "w_out": w_out}


def rotate(values, positions):
    half = values.shape[-1] // 2
    freqs = 500000.0 ** (-jnp.arange(half, dtype=jnp.float32) * 2.0 / values.shape[-1])
    angles = positions.astype(jnp.float32)[..., None] * freqs
    cosine = jnp.cos(angles)
    sine = jnp.sin(angles)
    first = values[..., :half]
    second = values[..., half:]
    return jnp.concatenate([first * cosine - second * sine, second * cosine + first * sine], -1)

def reference(hidden_states, norm_gain, w_query, w_key, w_value, cache, w_out):
    tokens = hidden_states.shape[0]
    prefix = cache.shape[0]
    group_size = HEADS // KV_HEADS
    states = hidden_states.astype(jnp.float32)
    normed = (states * lax.rsqrt(lax.optimization_barrier(jnp.mean(states * states, axis=1, keepdims=True)) + 1e-05) * norm_gain.astype(jnp.float32)).astype(jnp.bfloat16)
    positions = prefix + jnp.arange(tokens, dtype=jnp.int32)
    query = jnp.dot(normed, w_query, preferred_element_type=jnp.float32).reshape(tokens, HEADS, HEAD_DIM)
    query = rotate(query, positions[:, None]).astype(jnp.bfloat16)
    key_new = jnp.dot(normed, w_key, preferred_element_type=jnp.float32).reshape(tokens, KV_HEADS, HEAD_DIM)
    key_new = rotate(key_new, positions[:, None]).astype(jnp.bfloat16)
    value_new = jnp.dot(normed, w_value, preferred_element_type=jnp.float32).astype(jnp.bfloat16).reshape(tokens, KV_HEADS, HEAD_DIM)
    cache_heads = cache.reshape(prefix, KV_HEADS, 2, HEAD_DIM)
    keys = jnp.concatenate([cache_heads[:, :, 0], key_new], 0).transpose(1, 0, 2)
    values = jnp.concatenate([cache_heads[:, :, 1], value_new], 0).transpose(1, 0, 2)
    q_heads = query.reshape(tokens, KV_HEADS, group_size, HEAD_DIM).transpose(1, 0, 2, 3)
    blocks = tokens // ROWS
    scale = 1.0 / math.sqrt(HEAD_DIM)
    key_index = jnp.arange(prefix + tokens, dtype=jnp.int32) - prefix

    def head(item):
        q_head, k_head, v_head = item
        q_blocks = q_head.reshape(blocks, ROWS * group_size, HEAD_DIM)

        def block(item2):
            q_block, index = item2
            scores = lax.dot_general(q_block, k_head, (((1,), (1,)), ((), ())), preferred_element_type=jnp.float32) * scale
            query_pos = index * ROWS + jnp.arange(ROWS * group_size, dtype=jnp.int32) // group_size
            scores = jnp.where(key_index[None, :] <= query_pos[:, None], scores, -1e+30)
            top = lax.optimization_barrier(jnp.max(scores, axis=1, keepdims=True))
            weights = jnp.exp(scores - top)
            summed = jnp.dot(weights.astype(jnp.bfloat16), v_head, preferred_element_type=jnp.float32)
            return (summed / lax.optimization_barrier(jnp.sum(weights, axis=1, keepdims=True))).astype(jnp.bfloat16)
        return lax.map(block, (q_blocks, jnp.arange(blocks, dtype=jnp.int32)))
    attended = lax.map(head, (q_heads, keys, values))
    attended = attended.reshape(KV_HEADS, tokens, group_size, HEAD_DIM).transpose(1, 0, 2, 3).reshape(tokens, HEADS * HEAD_DIM)
    return jnp.dot(attended, w_out, preferred_element_type=jnp.float32).astype(jnp.bfloat16)
```

```python
import functools
import math

import jax
import jax.numpy as jnp
from jax import lax
from jax.experimental import pallas as pl
from jax.experimental.pallas import tpu as pltpu
from jax.sharding import PartitionSpec as P

HEAD_DIM = 128
MESH = pl.DeviceIdType.MESH
BF = jnp.bfloat16
F32 = jnp.float32
ROWS = 256
FEATURES = 8192
CHUNK = 256
NEG = -1e30
VMEM = pltpu.MemorySpace.VMEM


def place():
    grp = lax.axis_index("grp")
    tp = lax.axis_index("tp")
    return grp // 2, grp % 2, tp // 4, tp % 4


def wrap(i):
    return lax.rem(i + 8, 4)


def greet(partners):
    barrier = pltpu.get_barrier_semaphore()
    for partner in partners:
        pl.semaphore_signal(barrier, inc=1, device_id=partner, device_id_type=MESH)
    pl.semaphore_wait(barrier, len(partners))


def remote(src, dst, send, recv, partner):
    return pltpu.make_async_remote_copy(
        src_ref=src, dst_ref=dst, send_sem=send, recv_sem=recv, device_id=partner, device_id_type=MESH
    )


def project_kernel(
    hid, gain, cos, sin, wq_hbm, wk_hbm, wv_hbm, cache,
    q_out, kv_out,
    got, wq, wk, wv, acc, squares, part, partner_part, fresh,
    send, recv, load, swap_send, swap_recv,
):
    x, core, z, y = place()
    grp = 2 * x + core
    parity = lax.rem(y, 2)

    def at(dz, dy):
        return wrap(z + dz) * 4 + wrap(y + dy)

    def to(dz, dy):
        return {"grp": grp, "tp": at(dz, dy)}

    def chunk(half, a, b):
        return 2 * (at(b, a) if half == 0 else at(a, b)) + half

    def first(half, d):
        return to(0, d) if half == 0 else to(d, 0)

    def second(half, d):
        return to(d, 0) if half == 0 else to(0, d)

    partner = {"grp": grp, "tp": z * 4 + y + 1 - 2 * parity}
    sibling = {"grp": grp + 1 - 2 * core, "tp": z * 4 + y}
    loads = [
        pltpu.make_async_copy(wq_hbm, wq, load.at[0]),
        pltpu.make_async_copy(wk_hbm, wk, load.at[1]),
        pltpu.make_async_copy(wv_hbm, wv, load.at[2]),
    ]
    for one in loads:
        one.start()
    own_cache = pltpu.make_async_copy(cache, kv_out.at[parity, core, pl.ds(0, 2048)], load.at[3])
    own_cache.start()
    for half in range(2):
        got[chunk(half, 0, 0)] = hid[:, half * CHUNK : (half + 1) * CHUNK]
    greet([to(0, 1), to(0, -1), to(1, 0), to(-1, 0), sibling])

    TOP, BOTTOM, ALL = pl.ds(0, 128), pl.ds(128, 128), pl.ds(0, 256)

    def message(half, m, idx, rows, partner):
        ref = got.at[idx, rows]
        return remote(ref, ref, send.at[half, m], recv.at[half, m], partner)

    for m, d in ((0, 1), (1, -1)):
        for half in range(2):
            message(half, m, chunk(half, 0, 0), ALL, first(half, d)).start()
    for m, d in ((4, 1), (5, -1)):
        for half in range(2):
            message(half, m, chunk(half, 0, 0), ALL, second(half, d)).start()
    mine = kv_out.at[parity, core, pl.ds(0, 2048)]
    swaps = [
        remote(cache, mine, swap_send.at[0], swap_recv.at[0], partner),
        remote(cache, mine, swap_send.at[1], swap_recv.at[1], sibling),
    ]
    for one in swaps:
        one.start()

    acc[...] = jnp.zeros_like(acc)
    squares[...] = jnp.zeros_like(squares)

    def absorb(idx):
        h = got[idx].astype(F32)
        sq = h * h
        squares[...] += sq[:, :128] + sq[:, 128:]
        scaled = (h * gain[pl.ds(idx, 1), :]).astype(BF)
        depth = pl.ds(pl.multiple_of(idx * CHUNK, CHUNK), CHUNK)
        acc[:, :512] += jnp.dot(scaled, wq[depth, :], preferred_element_type=F32)
        wkv = jnp.concatenate([wk[depth, :], wv[depth, :]], axis=1)
        acc[:, 512:] += jnp.dot(scaled, wkv, preferred_element_type=F32)

    def absorb_all(count, index_of):
        def step(i, carry):
            absorb(index_of(i))
            return carry

        lax.fori_loop(0, count, step, 0)

    def pick(flag, a, b):
        return jnp.where(flag == 0, a, b)

    def chunk_of(half, a, b):
        return pick(half, chunk(0, a, b), chunk(1, a, b))

    def arrived(half, m, idx, rows):
        message(half, m, idx, rows, sibling).wait_recv()

    def spread(half, j, idx):
        message(half, 4 + 4 * j, idx, ALL, second(half, 1)).start()
        message(half, 5 + 4 * j, idx, ALL, second(half, -1)).start()

    for one in loads:
        one.wait()
    absorb_all(2, lambda i: chunk_of(i, 0, 0))
    for half in range(2):
        idx = chunk(half, -1, 0)
        arrived(half, 0, idx, ALL)
        message(half, 2, idx, TOP, first(half, 1)).start()
        spread(half, 1, idx)
    for half in range(2):
        idx = chunk(half, 1, 0)
        arrived(half, 1, idx, ALL)
        message(half, 3, idx, BOTTOM, first(half, -1)).start()
        spread(half, 2, idx)
    absorb_all(4, lambda i: chunk_of(i % 2, 2 * (i // 2) - 1, 0))

    def neighbours(j, a):
        for half in range(2):
            idx = chunk(half, a, -1)
            arrived(half, 4 + 4 * j, idx, ALL)
            message(half, 6 + 4 * j, idx, TOP, second(half, 1)).start()
            idx = chunk(half, a, 1)
            arrived(half, 5 + 4 * j, idx, ALL)
            message(half, 7 + 4 * j, idx, BOTTOM, second(half, -1)).start()
        absorb_all(4, lambda i: chunk_of(i % 2, a, 2 * (i // 2) - 1))

    def opposite(j, a):
        for half in range(2):
            idx = chunk(half, a, 2)
            arrived(half, 6 + 4 * j, idx, TOP)
            arrived(half, 7 + 4 * j, idx, BOTTOM)
        absorb_all(2, lambda i: chunk_of(i, a, 2))

    neighbours(0, 0)
    for half in range(2):
        idx = chunk(half, 2, 0)
        arrived(half, 2, idx, TOP)
        arrived(half, 3, idx, BOTTOM)
        spread(half, 3, idx)
    absorb_all(2, lambda i: chunk_of(i, 2, 0))

    def sweep(j, carry):
        neighbours(j, jnp.where(j == 1, -1, j - 1))
        return carry

    lax.fori_loop(1, 4, sweep, 0)
    theirs = kv_out.at[1 - parity, core, pl.ds(0, 2048)]
    remote(cache, theirs, swap_send.at[0], swap_recv.at[0], partner).wait_recv()
    passed = remote(theirs, theirs, swap_send.at[2], swap_recv.at[2], sibling)
    passed.start()

    def sweep_far(j, carry):
        opposite(j, jnp.where(j == 0, 0, jnp.where(j == 1, -1, j - 1)))
        return carry

    lax.fori_loop(0, 4, sweep_far, 0)

    mean = jnp.sum(squares[...], axis=1, keepdims=True) * (1.0 / FEATURES)
    root = lax.rsqrt(mean + 1e-05)
    lane = lax.broadcasted_iota(jnp.int32, (ROWS, 128), 1)
    own = acc[:, 512:] * root
    part[...] = own.astype(BF)
    swap = remote(part, partner_part, swap_send.at[3], swap_recv.at[3], partner)
    swap.start()
    c, s = cos[...], sin[...]

    def rope(v):
        return v * c + pltpu.roll(v, 64, 1) * s

    scale = math.log2(math.e) / math.sqrt(HEAD_DIM)
    parts = q_out.shape[0]
    tokens = ROWS // parts
    for head in range(4):
        turned = (rope(acc[:, head * 128 : (head + 1) * 128] * root) * scale).astype(BF)
        for i in range(parts):
            q_out[i, head * tokens : (head + 1) * tokens, :] = turned[i * tokens : (i + 1) * tokens, :]
    swap.wait()
    other = partner_part[...].astype(F32)
    left = jnp.where(parity == 0, own, other)
    right = jnp.where(parity == 0, other, own)
    key = jnp.where(lane < 64, left, pltpu.roll(right, 64, 1))
    value = jnp.where(lane < 64, pltpu.roll(left, 64, 1), right)
    fresh[0] = rope(key).astype(BF)
    fresh[1] = value.astype(BF)
    spot = kv_out.at[:, core, pl.ds(2048, 256)]
    keep = pltpu.make_async_copy(fresh, spot, load.at[0])
    keep.start()
    give = remote(fresh, spot, swap_send.at[4], swap_recv.at[4], sibling)
    give.start()
    keep.wait()
    give.wait_send()
    remote(fresh, kv_out.at[:, 1 - core, pl.ds(2048, 256)], swap_send.at[4], swap_recv.at[4], sibling).wait_recv()
    own_cache.wait()
    swaps[0].wait_send()
    swaps[1].wait_send()
    remote(cache, kv_out.at[parity, 1 - core, pl.ds(0, 2048)], swap_send.at[1], swap_recv.at[1], sibling).wait_recv()
    passed.wait_send()
    remote(
        cache, kv_out.at[1 - parity, 1 - core, pl.ds(0, 2048)], swap_send.at[2], swap_recv.at[2], sibling
    ).wait_recv()

    def drain(half, m, rows):
        message(half, m, chunk(half, 0, 0), rows, sibling).wait_send()

    for half in range(2):
        drain(half, 0, ALL)
        drain(half, 1, ALL)
        drain(half, 2, TOP)
        drain(half, 3, BOTTOM)
        for j in range(4):
            drain(half, 4 + 4 * j, ALL)
            drain(half, 5 + 4 * j, ALL)
            drain(half, 6 + 4 * j, TOP)
            drain(half, 7 + 4 * j, BOTTOM)


def project(hid, gain, cos, sin, wq, wk, wv, cache, parts):
    whole = pl.BlockSpec(memory_space=VMEM)
    left = pl.BlockSpec(memory_space=pl.ANY)
    dma = pltpu.SemaphoreType.DMA
    return pl.pallas_call(
        project_kernel,
        out_shape=(
            jax.ShapeDtypeStruct((parts, 1024 // parts, 128), BF),
            jax.ShapeDtypeStruct((2, 2, 2304, 128), BF),
        ),
        in_specs=[whole] * 4 + [left] * 4,
        out_specs=(whole, left),
        scratch_shapes=[
            pltpu.VMEM((32, ROWS, CHUNK), BF),
            pltpu.VMEM((FEATURES, 512), BF),
            pltpu.VMEM((FEATURES, 64), BF),
            pltpu.VMEM((FEATURES, 64), BF),
            pltpu.VMEM((ROWS, 640), F32),
            pltpu.VMEM((ROWS, 128), F32),
            pltpu.VMEM((ROWS, 128), BF),
            pltpu.VMEM((ROWS, 128), BF),
            pltpu.VMEM((2, ROWS, 128), BF),
            dma((2, 20)),
            dma((2, 20)),
            dma((4,)),
            dma((5,)),
            dma((5,)),
        ],
        compiler_params=pltpu.CompilerParams(
            collective_id=0, has_side_effects=True, vmem_limit_bytes=60 << 20
        ),
        name="project",
    )(hid, gain, cos, sin, wq, wk, wv, cache)


PIECES = ((0, 1024), (1024, 1024), (2048, 256))


def attend_kernel(
    q, kv, att,
    qs, ob, oin, stat, stat_in, sa, sb, top_a, top_b, summed, total,
    q_send, q_recv, o_send, o_recv, t_send, t_recv,
):
    x, core, z, y = place()
    tp = z * 4 + y
    parts, rows, width = q.shape
    tokens = rows // 4

    def chip(i):
        return {"grp": 2 * wrap(i) + core, "tp": tp}

    greet([chip(x + 1), chip(x + 2), chip(x + 3)])
    order = (1, 3, 2)

    def query(c, d):
        return remote(q.at[c], qs.at[d, c], q_send.at[d, c], q_recv.at[d, c], chip(x + d))

    for c in range(parts):
        for d in order:
            query(c, d).start()
    qs[0] = q[...]
    diff = lax.broadcasted_iota(jnp.int32, (rows, 256), 1) - lax.rem(
        lax.broadcasted_iota(jnp.int32, (rows, 256), 0), tokens
    )

    def block_of(i):
        c, k = i // 4, lax.rem(i, 4)
        k = jnp.where(c == 0, k, lax.rem(k + 1, 4))
        return c, jnp.where(k == 2, 3, jnp.where(k == 3, 2, k))

    def prepare(i):
        c, slot = block_of(i)

        @pl.when(slot != 0)
        def _():
            remote(q.at[0], qs.at[slot, c], q_send.at[slot, c], q_recv.at[slot, c], chip(x + 1)).wait_recv()

    def score(i, n, s_ref, top_ref):
        c, slot = block_of(i)
        b, (start, size) = n // 3, PIECES[n % 3]
        s = lax.dot_general(
            qs[slot, c], kv[0, b, start : start + size, :], (((1,), (1,)), ((), ())), preferred_element_type=F32
        )
        if size == 256:
            ahead = (2 * wrap(x - slot) + core - 2 * x - b) * ROWS + c * tokens
            s = jnp.where(diff <= ahead, s, NEG)
        s_ref[:, b * 2304 + start : b * 2304 + start + size] = s
        top = s[:, :128]
        for k in range(1, size // 128):
            top = jnp.maximum(top, s[:, k * 128 : (k + 1) * 128])
        top_ref[...] = top if n == 0 else jnp.maximum(top_ref[...], top)

    def weigh(n, s_ref, best):
        b, (start, size) = n // 3, PIECES[n % 3]
        s = s_ref[:, b * 2304 + start : b * 2304 + start + size]
        w = jnp.exp2(s - best)
        t = w[:, :128]
        for k in range(1, size // 128):
            t = t + w[:, k * 128 : (k + 1) * 128]
        o = jnp.dot(w.astype(BF), kv[1, b, start : start + size, :], preferred_element_type=F32)
        if n == 0:
            total[...] = t
            summed[...] = o
        else:
            total[...] += t
            summed[...] += o

    lane = lax.broadcasted_iota(jnp.int32, (rows, 128), 1)

    def settle(i, best):
        c, slot = block_of(i)
        ob[slot, c] = summed[...].astype(BF)
        t = jnp.sum(total[...], axis=1, keepdims=True)
        both = jnp.where(lane == 0, best, t)
        stat[slot, c] = both.T[:8, :]

        @pl.when(slot != 0)
        def _():
            home = chip(x - slot)
            remote(ob.at[slot, c], oin.at[slot, c], o_send.at[slot, c], o_recv.at[slot, c], home).start()
            remote(stat.at[slot, c], stat_in.at[slot, c], t_send.at[slot, c], t_recv.at[slot, c], home).start()

    def finish(c):
        for d in order:
            remote(ob.at[d, c], oin.at[d, c], o_send.at[d, c], o_recv.at[d, c], chip(x + 1)).wait_recv()
            remote(stat.at[d, c], stat_in.at[d, c], t_send.at[d, c], t_recv.at[d, c], chip(x + 1)).wait_recv()
        stats = [stat[0, c], stat_in[1, c], stat_in[2, c], stat_in[3, c]]
        tops = [s[0:1, :] for s in stats]
        peak = jnp.maximum(jnp.maximum(tops[0], tops[1]), jnp.maximum(tops[2], tops[3]))
        factors = [jnp.exp2(t - peak) for t in tops]
        whole = sum(f * s[1:2, :] for f, s in zip(factors, stats))
        inverse = 1.0 / whole
        row = lax.broadcasted_iota(jnp.int32, (128, rows), 0)
        table = jnp.zeros((128, rows), F32)
        for d in range(4):
            table = jnp.where(row == d, factors[d] * inverse, table)
        columns = table.T
        out = ob[0, c].astype(F32) * columns[:, 0:1]
        for d in range(1, 4):
            out = out + oin[d, c].astype(F32) * columns[:, d : d + 1]
        out = out.astype(BF)
        place_ = pl.ds(pl.multiple_of(c * tokens, tokens), tokens)
        for head in range(4):
            att[place_, head * 128 : (head + 1) * 128] = out[head * tokens : (head + 1) * tokens, :]

    blocks = 4 * parts
    prepare(0)
    for n in range(6):
        score(0, n, sa, top_a)

    def half_step(i, now, top_now, later, top_later):
        nxt = jnp.minimum(i + 1, blocks - 1)

        @pl.when(i + 1 < blocks)
        def _():
            prepare(nxt)

        best = jnp.max(top_now[...], axis=1, keepdims=True)
        for n in range(6):
            score(nxt, n, later, top_later)
            weigh(n, now, best)
        settle(i, best)

    def step(p, carry):
        half_step(2 * p, sa, top_a, sb, top_b)
        half_step(2 * p + 1, sb, top_b, sa, top_a)
        return carry

    lax.fori_loop(0, blocks // 2, step, 0)
    for c in range(parts):
        finish(c)
    for c in range(parts):
        for d in order:
            query(c, d).wait_send()
            remote(ob.at[d, c], oin.at[d, c], o_send.at[d, c], o_recv.at[d, c], chip(x + 1)).wait_send()
            remote(stat.at[d, c], stat_in.at[d, c], t_send.at[d, c], t_recv.at[d, c], chip(x + 1)).wait_send()


def attend(q, kv):
    parts, rows, width = q.shape
    whole = pl.BlockSpec(memory_space=VMEM)
    dma = pltpu.SemaphoreType.DMA
    return pl.pallas_call(
        attend_kernel,
        out_shape=jax.ShapeDtypeStruct((ROWS, 512), BF),
        in_specs=[whole] * 2,
        out_specs=whole,
        scratch_shapes=[
            pltpu.VMEM((4, parts, rows, 128), BF),
            pltpu.VMEM((4, parts, rows, 128), BF),
            pltpu.VMEM((4, parts, rows, 128), BF),
            pltpu.VMEM((4, parts, 8, rows), F32),
            pltpu.VMEM((4, parts, 8, rows), F32),
            pltpu.VMEM((rows, 4608), F32),
            pltpu.VMEM((rows, 4608), F32),
            pltpu.VMEM((rows, 128), F32),
            pltpu.VMEM((rows, 128), F32),
            pltpu.VMEM((rows, 128), F32),
            pltpu.VMEM((rows, 128), F32),
        ]
        + [dma((4, parts))] * 6,
        compiler_params=pltpu.CompilerParams(
            collective_id=1, has_side_effects=True, vmem_limit_bytes=60 << 20
        ),
        name="attend",
    )(q, kv)


def mix_kernel(att, w_hbm, out, w, terms, relay, inbox, terms2, relay2, inbox2, send, recv, load):
    x, core, z, y = place()
    grp = 2 * x + core
    rows = att.shape[0]
    half_rows = rows // 2

    def to(dz, dy):
        return {"grp": grp, "tp": wrap(z + dz) * 4 + wrap(y + dy)}

    def first(half, d):
        return to(0, d) if half == 0 else to(d, 0)

    def second(half, d):
        return to(d, 0) if half == 0 else to(0, d)

    here = ((y, z), (z, y))
    fetch = pltpu.make_async_copy(w_hbm, w, load.at[0])
    fetch.start()
    greet([to(0, 1), to(0, -1), to(1, 0), to(-1, 0)])
    fetch.wait()
    a_val = att[...]

    def fill(half, d):
        a = wrap(here[half][0] + d)

        def step(b, carry):
            t = b * 4 + a if half == 0 else a * 4 + b
            start = pl.multiple_of(t * 512 + half * 256, 256)
            r = jnp.dot(a_val, w[:, pl.ds(start, 256)], preferred_element_type=F32).astype(BF)
            terms[half, a, 0, b] = r[:half_rows]
            terms[half, a, 1, b] = r[half_rows:]
            return carry

        lax.fori_loop(0, 4, step, 0)

    def copy(half, m, src, dst, partner):
        return remote(src, dst, send.at[half, m], recv.at[half, m], partner)

    started = []

    def launch(*args):
        one = copy(*args)
        one.start()
        started.append(one)

    def add(dst, src):
        dst[...] = (dst[...].astype(F32) + src[...].astype(F32)).astype(BF)

    def block(half, d, ch):
        return terms.at[half, wrap(here[half][0] + d), ch]

    def block2(half, d, ch):
        return terms2.at[half, ch, wrap(here[half][1] + d)]

    for half in range(2):
        fill(half, 2)
        launch(half, 0, block(half, 2, 0), relay.at[half, 0], first(half, 1))
        launch(half, 1, block(half, 2, 1), relay.at[half, 1], first(half, -1))
    for half in range(2):
        fill(half, 1)
        launch(half, 2, block(half, 1, 1), inbox.at[half, 0, 1], first(half, 1))
        fill(half, -1)
        launch(half, 4, block(half, -1, 0), inbox.at[half, 1, 0], first(half, -1))
    for half in range(2):
        copy(half, 0, relay.at[half, 0], relay.at[half, 0], first(half, 1)).wait_recv()
        add(block(half, 1, 0), relay.at[half, 0])
        launch(half, 3, block(half, 1, 0), inbox.at[half, 0, 0], first(half, 1))
        copy(half, 1, relay.at[half, 1], relay.at[half, 1], first(half, 1)).wait_recv()
        add(block(half, -1, 1), relay.at[half, 1])
        launch(half, 5, block(half, -1, 1), inbox.at[half, 1, 1], first(half, -1))
    for half in range(2):
        fill(half, 0)
    for half in range(2):
        for m, side, ch in ((2, 0, 1), (4, 1, 0), (3, 0, 0), (5, 1, 1)):
            ref = inbox.at[half, side, ch]
            copy(half, m, ref, ref, first(half, 1)).wait_recv()

        def merge(b, carry):
            for ch in range(2):
                got = terms[half, here[half][0], ch, b].astype(F32)
                got = got + inbox[half, 0, ch, b].astype(F32) + inbox[half, 1, ch, b].astype(F32)
                terms2[half, ch, b] = got.astype(BF)
            return carry

        lax.fori_loop(0, 4, merge, 0)
        launch(half, 6, block2(half, 2, 0), relay2.at[half, 0], second(half, 1))
        launch(half, 7, block2(half, 2, 1), relay2.at[half, 1], second(half, -1))
        launch(half, 8, block2(half, 1, 1), inbox2.at[half, 0, 1], second(half, 1))
        launch(half, 10, block2(half, -1, 0), inbox2.at[half, 1, 0], second(half, -1))
    for half in range(2):
        copy(half, 6, relay2.at[half, 0], relay2.at[half, 0], first(half, 1)).wait_recv()
        add(block2(half, 1, 0), relay2.at[half, 0])
        launch(half, 9, block2(half, 1, 0), inbox2.at[half, 0, 0], second(half, 1))
        copy(half, 7, relay2.at[half, 1], relay2.at[half, 1], first(half, 1)).wait_recv()
        add(block2(half, -1, 1), relay2.at[half, 1])
        launch(half, 11, block2(half, -1, 1), inbox2.at[half, 1, 1], second(half, -1))
    for half in range(2):
        for m, side, ch in ((8, 0, 1), (10, 1, 0), (9, 0, 0), (11, 1, 1)):
            ref = inbox2.at[half, side, ch]
            copy(half, m, ref, ref, first(half, 1)).wait_recv()
        for ch in range(2):
            got = terms2[half, ch, here[half][1]].astype(F32)
            got = got + inbox2[half, 0, ch].astype(F32) + inbox2[half, 1, ch].astype(F32)
            out[ch * half_rows : (ch + 1) * half_rows, half * 256 : (half + 1) * 256] = got.astype(BF)
    for one in started:
        one.wait_send()


def mix(att, w_out):
    whole = pl.BlockSpec(memory_space=VMEM)
    dma = pltpu.SemaphoreType.DMA
    h = ROWS // 2
    return pl.pallas_call(
        mix_kernel,
        out_shape=jax.ShapeDtypeStruct((ROWS, 512), BF),
        in_specs=[whole, pl.BlockSpec(memory_space=pl.ANY)],
        out_specs=whole,
        scratch_shapes=[
            pltpu.VMEM((512, FEATURES), BF),
            pltpu.VMEM((2, 4, 2, 4, h, 256), BF),
            pltpu.VMEM((2, 2, 4, h, 256), BF),
            pltpu.VMEM((2, 2, 2, 4, h, 256), BF),
            pltpu.VMEM((2, 2, 4, h, 256), BF),
            pltpu.VMEM((2, 2, h, 256), BF),
            pltpu.VMEM((2, 2, 2, h, 256), BF),
            dma((2, 12)),
            dma((2, 12)),
            dma((1,)),
        ],
        compiler_params=pltpu.CompilerParams(
            collective_id=2, has_side_effects=True, vmem_limit_bytes=60 << 20
        ),
        name="mix",
    )(att, w_out)


def turns(first):
    half = HEAD_DIM // 2
    freqs = 500000.0 ** (-jnp.arange(half, dtype=F32) * 2.0 / HEAD_DIM)
    angles = (first + jnp.arange(ROWS, dtype=jnp.int32)).astype(F32)[:, None] * freqs
    cosine, sine = jnp.cos(angles), jnp.sin(angles)
    return jnp.concatenate([cosine, cosine], 1), jnp.concatenate([-sine, sine], 1)


def body(prefix, parts, hidden_states, norm_gain, w_query, w_key, w_value, cache, w_out):
    cos, sin = turns(prefix + lax.axis_index("grp") * ROWS)
    gain = norm_gain.reshape(FEATURES // CHUNK, CHUNK)
    q, kv = project(hidden_states, gain, cos, sin, w_query, w_key, w_value, cache, parts)
    return mix(attend(q, kv), w_out)


def solution(mesh):
    in_specs = (P("grp", "tp"), P(), P(None, "tp"), P(None, "tp"), P(None, "tp"), P("grp", "tp"), P("tp", None))
    return jax.shard_map(
        functools.partial(body, 16384, 2),
        mesh=mesh,
        in_specs=in_specs,
        out_specs=P("grp", "tp"),
        check_vma=False,
    )
```

```python
import functools
import math

import jax
import jax.numpy as jnp
import numpy as np
from jax import lax
from jax.experimental import pallas as pl
from jax.experimental.pallas import tpu as pltpu
from jax.sharding import PartitionSpec as P

HEAD_DIM = 128
MESH = pl.DeviceIdType.MESH
BF = jnp.bfloat16
F32 = jnp.float32
ROWS = 256
FEATURES = 8192
CHUNK = 256
NEG = -1e30
VMEM = pltpu.MemorySpace.VMEM


def place():
    grp = lax.axis_index("grp")
    tp = lax.axis_index("tp")
    return grp // 2, grp % 2, tp // 4, tp % 4


def wrap(i):
    return lax.rem(i + 8, 4)


def greet(partners):
    barrier = pltpu.get_barrier_semaphore()
    for partner in partners:
        pl.semaphore_signal(barrier, inc=1, device_id=partner, device_id_type=MESH)
    pl.semaphore_wait(barrier, len(partners))


def remote(src, dst, send, recv, partner):
    return pltpu.make_async_remote_copy(
        src_ref=src, dst_ref=dst, send_sem=send, recv_sem=recv, device_id=partner, device_id_type=MESH
    )


def project_kernel(
    prefix, hid, gain, freqs, wq_hbm, wk_hbm, wv_hbm, cache,
    q_out, kv_out,
    got, wq, wkv, acc, squares, cos, sin, part, partner_part, fresh,
    send, recv, load, swap_send, swap_recv,
):
    x, core, z, y = place()
    grp = 2 * x + core
    parity = lax.rem(y, 2)

    def at(dz, dy):
        return wrap(z + dz) * 4 + wrap(y + dy)

    def to(dz, dy):
        return {"grp": grp, "tp": at(dz, dy)}

    def chunk(half, a, b):
        return 2 * (at(b, a) if half == 0 else at(a, b)) + half

    def first(half, d):
        return to(0, d) if half == 0 else to(d, 0)

    def second(half, d):
        return to(d, 0) if half == 0 else to(0, d)

    partner = {"grp": grp, "tp": z * 4 + y + 1 - 2 * parity}
    sibling = {"grp": grp + 1 - 2 * core, "tp": z * 4 + y}
    loads = [
        pltpu.make_async_copy(wq_hbm, wq, load.at[0]),
        pltpu.make_async_copy(wk_hbm, wkv.at[pl.ds(0, 64)], load.at[1]),
        pltpu.make_async_copy(wv_hbm, wkv.at[pl.ds(64, 64)], load.at[2]),
    ]
    for one in loads:
        one.start()
    own_cache = pltpu.make_async_copy(cache, kv_out.at[parity, core, pl.ds(0, 2048)], load.at[3])
    own_cache.start()
    for half in range(2):
        got[chunk(half, 0, 0)] = hid[:, half * CHUNK : (half + 1) * CHUNK]
    greet([to(0, 1), to(0, -1), to(1, 0), to(-1, 0), sibling])

    TOP, BOTTOM, ALL = pl.ds(0, 128), pl.ds(128, 128), pl.ds(0, 256)

    def message(half, m, idx, rows, partner):
        ref = got.at[idx, rows]
        return remote(ref, ref, send.at[half, m], recv.at[half, m], partner)

    for m, d in ((0, 1), (1, -1)):
        for half in range(2):
            message(half, m, chunk(half, 0, 0), ALL, first(half, d)).start()
    for m, d in ((4, 1), (5, -1)):
        for half in range(2):
            message(half, m, chunk(half, 0, 0), ALL, second(half, d)).start()
    mine = kv_out.at[parity, core, pl.ds(0, 2048)]
    swaps = [
        remote(cache, mine, swap_send.at[0], swap_recv.at[0], partner),
        remote(cache, mine, swap_send.at[1], swap_recv.at[1], sibling),
    ]
    for one in swaps:
        one.start()

    acc[...] = jnp.zeros_like(acc)
    squares[...] = jnp.zeros_like(squares)

    def absorb(idx):
        h = got[idx].astype(F32)
        sq = h * h
        squares[...] += sq[:, :128] + sq[:, 128:]
        depth = pl.ds(pl.multiple_of(idx * CHUNK, CHUNK), CHUNK)
        scaled = (h * gain[:, depth]).astype(BF)
        acc[:, :512] += jnp.dot(scaled, wq[depth, :], preferred_element_type=F32)
        acc[:, 512:] += lax.dot_general(
            scaled, wkv[:, depth], (((1,), (1,)), ((), ())), preferred_element_type=F32
        )

    def absorb_all(count, index_of):
        def step(i, carry):
            absorb(index_of(i))
            return carry

        lax.fori_loop(0, count, step, 0)

    def pick(flag, a, b):
        return jnp.where(flag == 0, a, b)

    def chunk_of(half, a, b):
        return pick(half, chunk(0, a, b), chunk(1, a, b))

    def arrived(half, m, idx, rows):
        message(half, m, idx, rows, sibling).wait_recv()

    def spread(half, j, idx):
        message(half, 4 + 4 * j, idx, ALL, second(half, 1)).start()
        message(half, 5 + 4 * j, idx, ALL, second(half, -1)).start()

    lane = lax.broadcasted_iota(jnp.int32, (ROWS, 128), 1)
    row = lax.broadcasted_iota(jnp.int32, (ROWS, 128), 0)
    angles = (row + (prefix + grp * ROWS)).astype(F32) * freqs[...]
    cos[...] = jnp.cos(angles)
    sine = jnp.sin(angles)
    sin[...] = jnp.where(lane < 64, -sine, sine)
    for one in loads:
        one.wait()
    absorb_all(2, lambda i: chunk_of(i, 0, 0))
    for half in range(2):
        idx = chunk(half, -1, 0)
        arrived(half, 0, idx, ALL)
        message(half, 2, idx, TOP, first(half, 1)).start()
        spread(half, 1, idx)
    for half in range(2):
        idx = chunk(half, 1, 0)
        arrived(half, 1, idx, ALL)
        message(half, 3, idx, BOTTOM, first(half, -1)).start()
        spread(half, 2, idx)
    absorb_all(4, lambda i: chunk_of(i % 2, 2 * (i // 2) - 1, 0))

    def neighbours(j, a):
        for half in range(2):
            idx = chunk(half, a, -1)
            arrived(half, 4 + 4 * j, idx, ALL)
            message(half, 6 + 4 * j, idx, TOP, second(half, 1)).start()
            idx = chunk(half, a, 1)
            arrived(half, 5 + 4 * j, idx, ALL)
            message(half, 7 + 4 * j, idx, BOTTOM, second(half, -1)).start()
        absorb_all(4, lambda i: chunk_of(i % 2, a, 2 * (i // 2) - 1))

    def opposite(j, a):
        for half in range(2):
            idx = chunk(half, a, 2)
            arrived(half, 6 + 4 * j, idx, TOP)
            arrived(half, 7 + 4 * j, idx, BOTTOM)
        absorb_all(2, lambda i: chunk_of(i, a, 2))

    neighbours(0, 0)
    for half in range(2):
        idx = chunk(half, 2, 0)
        arrived(half, 2, idx, TOP)
        arrived(half, 3, idx, BOTTOM)
        spread(half, 3, idx)
    absorb_all(2, lambda i: chunk_of(i, 2, 0))

    def sweep(j, carry):
        neighbours(j, jnp.where(j == 1, -1, j - 1))
        return carry

    lax.fori_loop(1, 4, sweep, 0)
    theirs = kv_out.at[1 - parity, core, pl.ds(0, 2048)]
    remote(cache, theirs, swap_send.at[0], swap_recv.at[0], partner).wait_recv()
    passed = remote(theirs, theirs, swap_send.at[2], swap_recv.at[2], sibling)
    passed.start()

    def sweep_far(j, carry):
        opposite(j, jnp.where(j == 0, 0, jnp.where(j == 1, -1, j - 1)))
        return carry

    lax.fori_loop(0, 4, sweep_far, 0)

    mean = jnp.sum(squares[...], axis=1, keepdims=True) * (1.0 / FEATURES)
    root = lax.rsqrt(mean + 1e-05)
    own = acc[:, 512:] * root
    part[...] = own.astype(BF)
    swap = remote(part, partner_part, swap_send.at[3], swap_recv.at[3], partner)
    swap.start()
    c, s = cos[...], sin[...]

    def rope(v):
        return v * c + pltpu.roll(v, 64, 1) * s

    scale = math.log2(math.e) / math.sqrt(HEAD_DIM)
    parts = q_out.shape[0]
    tokens = ROWS // parts
    for head in range(4):
        turned = (rope(acc[:, head * 128 : (head + 1) * 128] * root) * scale).astype(BF)
        for i in range(parts):
            q_out[i, head * tokens : (head + 1) * tokens, :] = turned[i * tokens : (i + 1) * tokens, :]
    swap.wait()
    other = partner_part[...].astype(F32)
    left = jnp.where(parity == 0, own, other)
    right = jnp.where(parity == 0, other, own)
    key = jnp.where(lane < 64, left, pltpu.roll(right, 64, 1))
    value = jnp.where(lane < 64, pltpu.roll(left, 64, 1), right)
    fresh[0] = rope(key).astype(BF)
    fresh[1] = value.astype(BF)
    spot = kv_out.at[:, core, pl.ds(2048, 256)]
    keep = pltpu.make_async_copy(fresh, spot, load.at[0])
    keep.start()
    give = remote(fresh, spot, swap_send.at[4], swap_recv.at[4], sibling)
    give.start()
    keep.wait()
    give.wait_send()
    remote(fresh, kv_out.at[:, 1 - core, pl.ds(2048, 256)], swap_send.at[4], swap_recv.at[4], sibling).wait_recv()
    own_cache.wait()
    swaps[0].wait_send()
    swaps[1].wait_send()
    remote(cache, kv_out.at[parity, 1 - core, pl.ds(0, 2048)], swap_send.at[1], swap_recv.at[1], sibling).wait_recv()
    passed.wait_send()
    remote(
        cache, kv_out.at[1 - parity, 1 - core, pl.ds(0, 2048)], swap_send.at[2], swap_recv.at[2], sibling
    ).wait_recv()

    def drain(half, m, rows):
        message(half, m, chunk(half, 0, 0), rows, sibling).wait_send()

    for half in range(2):
        drain(half, 0, ALL)
        drain(half, 1, ALL)
        drain(half, 2, TOP)
        drain(half, 3, BOTTOM)
        for j in range(4):
            drain(half, 4 + 4 * j, ALL)
            drain(half, 5 + 4 * j, ALL)
            drain(half, 6 + 4 * j, TOP)
            drain(half, 7 + 4 * j, BOTTOM)


def project(hid, gain, wq, wk, wv, cache, prefix, parts):
    whole = pl.BlockSpec(memory_space=VMEM)
    left = pl.BlockSpec(memory_space=pl.ANY)
    dma = pltpu.SemaphoreType.DMA
    half = np.arange(HEAD_DIM // 2, dtype=np.float64) * 2.0 / HEAD_DIM
    freqs = jnp.asarray(np.tile(500000.0**-half, 2)[None, :], F32)
    return pl.pallas_call(
        functools.partial(project_kernel, prefix),
        out_shape=(
            jax.ShapeDtypeStruct((parts, 1024 // parts, 128), BF),
            jax.ShapeDtypeStruct((2, 2, 2304, 128), BF),
        ),
        in_specs=[whole] * 3 + [left] * 4,
        out_specs=(whole, left),
        scratch_shapes=[
            pltpu.VMEM((32, ROWS, CHUNK), BF),
            pltpu.VMEM((FEATURES, 512), BF),
            pltpu.VMEM((128, FEATURES), BF),
            pltpu.VMEM((ROWS, 640), F32),
            pltpu.VMEM((ROWS, 128), F32),
            pltpu.VMEM((ROWS, 128), F32),
            pltpu.VMEM((ROWS, 128), F32),
            pltpu.VMEM((ROWS, 128), BF),
            pltpu.VMEM((ROWS, 128), BF),
            pltpu.VMEM((2, ROWS, 128), BF),
            dma((2, 20)),
            dma((2, 20)),
            dma((4,)),
            dma((5,)),
            dma((5,)),
        ],
        compiler_params=pltpu.CompilerParams(
            collective_id=0, has_side_effects=True, vmem_limit_bytes=60 << 20
        ),
        name="project",
    )(hid, gain, freqs, wq, wk.T, wv.T, cache)


PIECES = ((0, 1024), (1024, 1024), (2048, 256))


def attend_mix_kernel(
    q, kv, w_hbm, out,
    w, vx, qs, ob, oin, stat, stat_in, sa, sb, top_a, top_b, summed, att,
    terms, relay, inbox, terms2, relay2, inbox2,
    q_send, q_recv, o_send, o_recv, t_send, t_recv, send, recv, load,
):
    x, core, z, y = place()
    grp = 2 * x + core
    tp = z * 4 + y
    parts, rows, width = q.shape
    tokens = rows // 4
    half_rows = tokens // 2

    def chip(i):
        return {"grp": 2 * wrap(i) + core, "tp": tp}

    def to(dz, dy):
        return {"grp": grp, "tp": wrap(z + dz) * 4 + wrap(y + dy)}

    def first(half, d):
        return to(0, d) if half == 0 else to(d, 0)

    def second(half, d):
        return to(d, 0) if half == 0 else to(0, d)

    here = ((y, z), (z, y))
    fetch = pltpu.make_async_copy(w_hbm, w, load.at[0])
    fetch.start()
    greet([chip(x + 1), chip(x + 2), chip(x + 3), to(0, 1), to(0, -1), to(1, 0), to(-1, 0)])
    order = (1, 3, 2)

    def query(c, d):
        return remote(q.at[c], qs.at[d, c], q_send.at[d, c], q_recv.at[d, c], chip(x + d))

    for c in range(parts):
        for d in order:
            query(c, d).start()
    qs[0] = q[...]
    for b in range(2):
        vx[b, :, :128] = kv[1, b]
        vx[b, :, 128:] = jnp.ones((2304, 128), BF)
    diff = lax.broadcasted_iota(jnp.int32, (rows, 256), 1) - lax.rem(
        lax.broadcasted_iota(jnp.int32, (rows, 256), 0), tokens
    )

    def block_of(i):
        c, k = i // 4, lax.rem(i, 4)
        k = jnp.where(c == 0, k, lax.rem(k + 1, 4))
        return c, jnp.where(k == 2, 3, jnp.where(k == 3, 2, k))

    def prepare(i):
        c, slot = block_of(i)

        @pl.when(slot != 0)
        def _():
            remote(q.at[0], qs.at[slot, c], q_send.at[slot, c], q_recv.at[slot, c], chip(x + 1)).wait_recv()

    def score(i, n, s_ref, top_ref):
        c, slot = block_of(i)
        b, (start, size) = n // 3, PIECES[n % 3]
        s = lax.dot_general(
            qs[slot, c], kv[0, b, start : start + size, :], (((1,), (1,)), ((), ())), preferred_element_type=F32
        )
        if size == 256:
            ahead = (2 * wrap(x - slot) + core - 2 * x - b) * ROWS + c * tokens
            s = jnp.where(diff <= ahead, s, NEG)
        s_ref[:, b * 2304 + start : b * 2304 + start + size] = s
        top = s[:, :128]
        for k in range(1, size // 128):
            top = jnp.maximum(top, s[:, k * 128 : (k + 1) * 128])
        top_ref[...] = top if n == 0 else jnp.maximum(top_ref[...], top)

    def weigh(n, s_ref, best):
        b, (start, size) = n // 3, PIECES[n % 3]
        w_ = jnp.exp2(s_ref[:, b * 2304 + start : b * 2304 + start + size] - best)
        o = jnp.dot(w_.astype(BF), vx[b, start : start + size, :], preferred_element_type=F32)
        summed[...] = o if n == 0 else summed[...] + o

    lane = lax.broadcasted_iota(jnp.int32, (rows, 128), 1)

    def settle(i, best):
        c, slot = block_of(i)
        ob[slot, c] = summed[:, :128].astype(BF)
        both = jnp.where(lane == 0, best, summed[:, 128:])
        stat[slot, c] = both.T[:8, :]

        @pl.when(slot != 0)
        def _():
            home = chip(x - slot)
            remote(ob.at[slot, c], oin.at[slot, c], o_send.at[slot, c], o_recv.at[slot, c], home).start()
            remote(stat.at[slot, c], stat_in.at[slot, c], t_send.at[slot, c], t_recv.at[slot, c], home).start()

    def finish(c):
        for d in order:
            remote(ob.at[d, c], oin.at[d, c], o_send.at[d, c], o_recv.at[d, c], chip(x + 1)).wait_recv()
            remote(stat.at[d, c], stat_in.at[d, c], t_send.at[d, c], t_recv.at[d, c], chip(x + 1)).wait_recv()
        stats = [stat[0, c], stat_in[1, c], stat_in[2, c], stat_in[3, c]]
        tops = [s[0:1, :] for s in stats]
        peak = jnp.maximum(jnp.maximum(tops[0], tops[1]), jnp.maximum(tops[2], tops[3]))
        factors = [jnp.exp2(t - peak) for t in tops]
        whole = sum(f * s[1:2, :] for f, s in zip(factors, stats))
        inverse = 1.0 / whole
        row = lax.broadcasted_iota(jnp.int32, (128, rows), 0)
        table = jnp.zeros((128, rows), F32)
        for d in range(4):
            table = jnp.where(row == d, factors[d] * inverse, table)
        columns = table.T
        o = ob[0, c].astype(F32) * columns[:, 0:1]
        for d in range(1, 4):
            o = o + oin[d, c].astype(F32) * columns[:, d : d + 1]
        o = o.astype(BF)
        for head in range(4):
            att[:, head * 128 : (head + 1) * 128] = o[head * tokens : (head + 1) * tokens, :]

    def fill(c, half, d):
        a = wrap(here[half][0] + d)

        def step(b, carry):
            t = b * 4 + a if half == 0 else a * 4 + b
            start = pl.multiple_of(t * 512 + half * 256, 256)
            r = jnp.dot(att[...], w[:, pl.ds(start, 256)], preferred_element_type=F32).astype(BF)
            terms[c, half, a, 0, b] = r[:half_rows]
            terms[c, half, a, 1, b] = r[half_rows:]
            return carry

        lax.fori_loop(0, 4, step, 0)

    def copy(c, half, m, src, dst, partner):
        return remote(src, dst, send.at[c, half, m], recv.at[c, half, m], partner)

    def moves(c, half):
        def block(d, ch):
            return terms.at[c, half, wrap(here[half][0] + d), ch]

        def block2(d, ch):
            return terms2.at[c, half, ch, wrap(here[half][1] + d)]

        ends = (
            (block(2, 0), relay.at[c, half, 0], first(half, 1)),
            (block(2, 1), relay.at[c, half, 1], first(half, -1)),
            (block(1, 1), inbox.at[c, half, 0, 1], first(half, 1)),
            (block(1, 0), inbox.at[c, half, 0, 0], first(half, 1)),
            (block(-1, 0), inbox.at[c, half, 1, 0], first(half, -1)),
            (block(-1, 1), inbox.at[c, half, 1, 1], first(half, -1)),
            (block2(2, 0), relay2.at[c, half, 0], second(half, 1)),
            (block2(2, 1), relay2.at[c, half, 1], second(half, -1)),
            (block2(1, 1), inbox2.at[c, half, 0, 1], second(half, 1)),
            (block2(1, 0), inbox2.at[c, half, 0, 0], second(half, 1)),
            (block2(-1, 0), inbox2.at[c, half, 1, 0], second(half, -1)),
            (block2(-1, 1), inbox2.at[c, half, 1, 1], second(half, -1)),
        )
        return (lambda m: copy(c, half, m, *ends[m])), ends

    def add(dst, src):
        dst[...] = (dst[...].astype(F32) + src[...].astype(F32)).astype(BF)

    def stage0(c):
        finish(c)
        for half in range(2):
            sends, _ = moves(c, half)
            fill(c, half, 2)
            sends(0).start()
            sends(1).start()
        for half in range(2):
            sends, _ = moves(c, half)
            fill(c, half, 1)
            sends(2).start()
            fill(c, half, -1)
            sends(4).start()
        for half in range(2):
            fill(c, half, 0)

    def stage1(c):
        for half in range(2):
            sends, ends = moves(c, half)
            for m, k in ((0, 3), (1, 5)):
                sends(m).wait_recv()
                add(ends[k][0], ends[m][1])
                sends(k).start()

    def stage2(c):
        for half in range(2):
            sends, _ = moves(c, half)
            for m in (2, 4, 3, 5):
                sends(m).wait_recv()

            def merge(b, carry):
                for ch in range(2):
                    got = terms[c, half, here[half][0], ch, b].astype(F32)
                    got = got + inbox[c, half, 0, ch, b].astype(F32) + inbox[c, half, 1, ch, b].astype(F32)
                    terms2[c, half, ch, b] = got.astype(BF)
                return carry

            lax.fori_loop(0, 4, merge, 0)
            for m in (6, 7, 8, 10):
                sends(m).start()

    def stage3(c):
        for half in range(2):
            sends, ends = moves(c, half)
            for m, k in ((6, 9), (7, 11)):
                sends(m).wait_recv()
                add(ends[k][0], ends[m][1])
                sends(k).start()

    def stage4(c):
        for half in range(2):
            sends, _ = moves(c, half)
            for m in (8, 10, 9, 11):
                sends(m).wait_recv()
            for ch in range(2):
                got = terms2[c, half, ch, here[half][1]].astype(F32)
                got = got + inbox2[c, half, 0, ch].astype(F32) + inbox2[c, half, 1, ch].astype(F32)
                start = c * tokens + ch * half_rows
                out[start : start + half_rows, half * 256 : (half + 1) * 256] = got.astype(BF)

    blocks = 4 * parts
    prepare(0)
    for n in range(6):
        score(0, n, sa, top_a)

    def half_step(i, now, top_now, later, top_later):
        nxt = jnp.minimum(i + 1, blocks - 1)

        @pl.when(i + 1 < blocks)
        def _():
            prepare(nxt)

        best = jnp.max(top_now[...], axis=1, keepdims=True)
        for n in range(6):
            score(nxt, n, later, top_later)
            weigh(n, now, best)
        settle(i, best)

    def step(p, carry):
        @pl.when(p == 3)
        def _():
            stage1(0)

        half_step(2 * p, sa, top_a, sb, top_b)

        @pl.when(p == 2)
        def _():
            fetch.wait()
            stage0(0)

        @pl.when(p == 3)
        def _():
            stage2(0)

        half_step(2 * p + 1, sb, top_b, sa, top_a)
        return carry

    lax.fori_loop(0, blocks // 2, step, 0)
    stage3(0)
    stage0(1)
    stage4(0)
    stage1(1)
    stage2(1)
    stage3(1)
    stage4(1)
    for c in range(parts):
        for d in order:
            query(c, d).wait_send()
            remote(ob.at[d, c], oin.at[d, c], o_send.at[d, c], o_recv.at[d, c], chip(x + 1)).wait_send()
            remote(stat.at[d, c], stat_in.at[d, c], t_send.at[d, c], t_recv.at[d, c], chip(x + 1)).wait_send()
        for half in range(2):
            sends, _ = moves(c, half)
            for m in range(12):
                sends(m).wait_send()


def attend_mix(q, kv, w_out):
    parts, rows, width = q.shape
    whole = pl.BlockSpec(memory_space=VMEM)
    dma = pltpu.SemaphoreType.DMA
    h = rows // 8
    return pl.pallas_call(
        attend_mix_kernel,
        out_shape=jax.ShapeDtypeStruct((ROWS, 512), BF),
        in_specs=[whole, whole, pl.BlockSpec(memory_space=pl.ANY)],
        out_specs=whole,
        scratch_shapes=[
            pltpu.VMEM((512, FEATURES), BF),
            pltpu.VMEM((2, 2304, 256), BF),
            pltpu.VMEM((4, parts, rows, 128), BF),
            pltpu.VMEM((4, parts, rows, 128), BF),
            pltpu.VMEM((4, parts, rows, 128), BF),
            pltpu.VMEM((4, parts, 8, rows), F32),
            pltpu.VMEM((4, parts, 8, rows), F32),
            pltpu.VMEM((rows, 4608), F32),
            pltpu.VMEM((rows, 4608), F32),
            pltpu.VMEM((rows, 128), F32),
            pltpu.VMEM((rows, 128), F32),
            pltpu.VMEM((rows, 256), F32),
            pltpu.VMEM((rows // 4, 512), BF),
            pltpu.VMEM((parts, 2, 4, 2, 4, h, 256), BF),
            pltpu.VMEM((parts, 2, 2, 4, h, 256), BF),
            pltpu.VMEM((parts, 2, 2, 2, 4, h, 256), BF),
            pltpu.VMEM((parts, 2, 2, 4, h, 256), BF),
            pltpu.VMEM((parts, 2, 2, h, 256), BF),
            pltpu.VMEM((parts, 2, 2, 2, h, 256), BF),
        ]
        + [dma((4, parts))] * 6
        + [dma((parts, 2, 12)), dma((parts, 2, 12)), dma((1,))],
        compiler_params=pltpu.CompilerParams(
            collective_id=1, has_side_effects=True, vmem_limit_bytes=60 << 20
        ),
        name="attend_mix",
    )(q, kv, w_out)


def body(prefix, parts, hidden_states, norm_gain, w_query, w_key, w_value, cache, w_out):
    gain = norm_gain.reshape(1, FEATURES)
    q, kv = project(hidden_states, gain, w_query, w_key, w_value, cache, prefix, parts)
    return attend_mix(q, kv, w_out)


def solution(mesh):
    in_specs = (P("grp", "tp"), P(), P(None, "tp"), P(None, "tp"), P(None, "tp"), P("grp", "tp"), P("tp", None))
    return jax.shard_map(
        functools.partial(body, 16384, 2),
        mesh=mesh,
        in_specs=in_specs,
        out_specs=P("grp", "tp"),
        check_vma=False,
    )
```

```python
import functools
import math

import jax
import jax.numpy as jnp
import numpy as np
from jax import lax
from jax.experimental import pallas as pl
from jax.experimental.pallas import tpu as pltpu
from jax.sharding import PartitionSpec as P

HEAD_DIM = 128
MESH = pl.DeviceIdType.MESH
BF = jnp.bfloat16
F32 = jnp.float32
ROWS = 256
FEATURES = 8192
CUTS = ((0, 384), (384, 128))
PIECES = ((0, 0, 1024), (0, 1024, 1024), (1, 0, 1024), (1, 1024, 1024), (0, 2048, 256), (1, 2048, 256))
NEG = -1e30
VMEM = pltpu.MemorySpace.VMEM


def place():
    grp = lax.axis_index("grp")
    tp = lax.axis_index("tp")
    return grp // 2, grp % 2, tp // 4, tp % 4


def wrap(i):
    return lax.rem(i + 8, 4)


def greet(partners):
    barrier = pltpu.get_barrier_semaphore()
    for partner in partners:
        pl.semaphore_signal(barrier, inc=1, device_id=partner, device_id_type=MESH)
    pl.semaphore_wait(barrier, len(partners))


def remote(src, dst, send, recv, partner):
    return pltpu.make_async_remote_copy(
        src_ref=src, dst_ref=dst, send_sem=send, recv_sem=recv, device_id=partner, device_id_type=MESH
    )


def block_kernel(
    prefix, parts, hid, gain, freqs, wq_hbm, wk_hbm, wv_hbm, cache, w_hbm,
    out,
    got_a, got_b, w, wkv, acc, squares, cos, sin, part, partner_part, fresh, kv, vx,
    qs, ob, oin, stat, stat_in, sa, sb, top_a, top_b, summed, att,
    terms, relay, inbox, terms2, relay2, inbox2,
    send, recv, load, w_load, swap_send, swap_recv,
    q_send, q_recv, o_send, o_recv, t_send, t_recv, r_send, r_recv,
):
    got = (got_a, got_b)
    tokens = ROWS // parts
    rows = 4 * tokens
    half_rows = tokens // 2
    x, core, z, y = place()
    grp = 2 * x + core
    parity = lax.rem(y, 2)

    def at(dz, dy):
        return wrap(z + dz) * 4 + wrap(y + dy)

    def to(dz, dy):
        return {"grp": grp, "tp": at(dz, dy)}

    def chip(i):
        return {"grp": 2 * wrap(i) + core, "tp": z * 4 + y}

    def chunk(half, a, b):
        return at(b, a) if half == 0 else at(a, b)

    def first(half, d):
        return to(0, d) if half == 0 else to(d, 0)

    def second(half, d):
        return to(d, 0) if half == 0 else to(0, d)

    partner = {"grp": grp, "tp": z * 4 + y + 1 - 2 * parity}
    sibling = {"grp": grp + 1 - 2 * core, "tp": z * 4 + y}
    loads = [
        pltpu.make_async_copy(wq_hbm, w, load.at[0]),
        pltpu.make_async_copy(wk_hbm, wkv.at[pl.ds(0, 64)], load.at[1]),
        pltpu.make_async_copy(wv_hbm, wkv.at[pl.ds(64, 64)], load.at[2]),
    ]
    for one in loads:
        one.start()
    own_cache = pltpu.make_async_copy(cache, kv.at[parity, core, pl.ds(0, 2048)], load.at[3])
    own_cache.start()
    for half, (start, size) in enumerate(CUTS):
        got[half][at(0, 0)] = hid[:, start : start + size]
    order = (1, 3, 2)
    greet([to(0, 1), to(0, -1), to(1, 0), to(-1, 0), sibling, chip(x + 1), chip(x + 2), chip(x + 3)])

    TOP, BOTTOM, ALL = pl.ds(0, 128), pl.ds(128, 128), pl.ds(0, 256)

    def message(half, m, idx, rows, partner):
        ref = got[half].at[idx, rows]
        return remote(ref, ref, send.at[half, m], recv.at[half, m], partner)

    for m, d in ((0, 1), (1, -1)):
        for half in range(2):
            message(half, m, chunk(half, 0, 0), ALL, first(half, d)).start()
    for m, d in ((4, 1), (5, -1)):
        for half in range(2):
            message(half, m, chunk(half, 0, 0), ALL, second(half, d)).start()
    acc[...] = jnp.zeros_like(acc)
    vx[:, :, 128:] = jnp.ones((2, 2304, 128), BF)
    squares[...] = jnp.zeros_like(squares)

    def absorb(half, t):
        offset, size = CUTS[half]
        h = got[half][t].astype(F32)
        sq = h * h
        sums = sq[:, :128]
        for k in range(1, size // 128):
            sums = sums + sq[:, k * 128 : (k + 1) * 128]
        squares[...] += sums
        depth = pl.ds(pl.multiple_of(t * 512 + offset, 128), size)
        scaled = (h * gain[:, depth]).astype(BF)
        acc[:, :512] += jnp.dot(scaled, w[depth, :], preferred_element_type=F32)
        acc[:, 512:] += lax.dot_general(
            scaled, wkv[:, depth], (((1,), (1,)), ((), ())), preferred_element_type=F32
        )

    def absorb_all(count, place_of):
        def step(i, carry):
            for half in range(2):
                absorb(half, chunk(half, *place_of(i)))
            return carry

        lax.fori_loop(0, count, step, 0)

    def arrived(half, m, idx, rows):
        message(half, m, idx, rows, sibling).wait_recv()

    def spread(half, j, idx):
        message(half, 4 + 4 * j, idx, ALL, second(half, 1)).start()
        message(half, 5 + 4 * j, idx, ALL, second(half, -1)).start()

    lane = lax.broadcasted_iota(jnp.int32, (ROWS, 128), 1)
    row = lax.broadcasted_iota(jnp.int32, (ROWS, 128), 0)
    angles = (row + (prefix + grp * ROWS)).astype(F32) * freqs[...]
    cos[...] = jnp.cos(angles)
    sine = jnp.sin(angles)
    sin[...] = jnp.where(lane < 64, -sine, sine)
    for one in loads:
        one.wait()
    absorb_all(1, lambda i: (0, 0))
    for half in range(2):
        idx = chunk(half, -1, 0)
        arrived(half, 0, idx, ALL)
        message(half, 2, idx, TOP, first(half, 1)).start()
        spread(half, 1, idx)
    for half in range(2):
        idx = chunk(half, 1, 0)
        arrived(half, 1, idx, ALL)
        message(half, 3, idx, BOTTOM, first(half, -1)).start()
        spread(half, 2, idx)
    mine = kv.at[parity, core, pl.ds(0, 2048)]
    swaps = [
        remote(cache, mine, swap_send.at[0], swap_recv.at[0], partner),
        remote(cache, mine, swap_send.at[1], swap_recv.at[1], sibling),
    ]
    for one in swaps:
        one.start()
    absorb_all(2, lambda i: (2 * i - 1, 0))

    def neighbours(j, a):
        for half in range(2):
            idx = chunk(half, a, -1)
            arrived(half, 4 + 4 * j, idx, ALL)
            message(half, 6 + 4 * j, idx, TOP, second(half, 1)).start()
            idx = chunk(half, a, 1)
            arrived(half, 5 + 4 * j, idx, ALL)
            message(half, 7 + 4 * j, idx, BOTTOM, second(half, -1)).start()
        absorb_all(2, lambda i: (a, 2 * i - 1))

    def opposite(j, a):
        for half in range(2):
            idx = chunk(half, a, 2)
            arrived(half, 6 + 4 * j, idx, TOP)
            arrived(half, 7 + 4 * j, idx, BOTTOM)
        absorb_all(1, lambda i: (a, 2))

    neighbours(0, 0)
    for half in range(2):
        idx = chunk(half, 2, 0)
        arrived(half, 2, idx, TOP)
        arrived(half, 3, idx, BOTTOM)
        spread(half, 3, idx)
    absorb_all(1, lambda i: (2, 0))

    def sweep(j, carry):
        neighbours(j, jnp.where(j == 1, -1, j - 1))
        return carry

    lax.fori_loop(1, 4, sweep, 0)
    theirs = kv.at[1 - parity, core, pl.ds(0, 2048)]
    remote(cache, theirs, swap_send.at[0], swap_recv.at[0], partner).wait_recv()
    passed = remote(theirs, theirs, swap_send.at[2], swap_recv.at[2], sibling)
    passed.start()

    def sweep_far(j, carry):
        opposite(j, jnp.where(j == 0, 0, jnp.where(j == 1, -1, j - 1)))
        return carry

    lax.fori_loop(0, 4, sweep_far, 0)

    mean = jnp.sum(squares[...], axis=1, keepdims=True) * (1.0 / FEATURES)
    root = lax.rsqrt(mean + 1e-05)
    own = acc[:, 512:] * root
    part[...] = own.astype(BF)
    swap = remote(part, partner_part, swap_send.at[3], swap_recv.at[3], partner)
    swap.start()
    def rope(v):
        return v * cos[...] + pltpu.roll(v, 64, 1) * sin[...]

    scale = math.log2(math.e) / math.sqrt(HEAD_DIM)
    for head in range(4):
        turned = (rope(acc[:, head * 128 : (head + 1) * 128] * root) * scale).astype(BF)
        for i in range(parts):
            qs[0, i, head * tokens : (head + 1) * tokens, :] = turned[i * tokens : (i + 1) * tokens, :]

    def query(c, d):
        return remote(qs.at[0, c], qs.at[d, c], q_send.at[d, c], q_recv.at[d, c], chip(x + d))

    for c in range(parts):
        for d in order:
            query(c, d).start()

    def fetch(t):
        spot = w.at[pl.ds(pl.multiple_of(t * 512, 512), 512)]
        return pltpu.make_async_copy(w_hbm.at[:, pl.ds(pl.multiple_of(t * 512, 512), 512)], spot, w_load.at[t])

    def begin(t, carry):
        fetch(t).start()
        return carry

    lax.fori_loop(0, 16, begin, 0)
    swap.wait()
    other = partner_part[...].astype(F32)
    left = jnp.where(parity == 0, own, other)
    right = jnp.where(parity == 0, other, own)
    key = jnp.where(lane < 64, left, pltpu.roll(right, 64, 1))
    value = jnp.where(lane < 64, pltpu.roll(left, 64, 1), right)
    fresh[0] = rope(key).astype(BF)
    fresh[1] = value.astype(BF)
    spot = kv.at[:, core, pl.ds(2048, 256)]
    keep = pltpu.make_async_copy(fresh, spot, load.at[0])
    keep.start()
    give = remote(fresh, spot, swap_send.at[4], swap_recv.at[4], sibling)
    give.start()
    own_cache.wait()
    remote(cache, kv.at[parity, 1 - core, pl.ds(0, 2048)], swap_send.at[1], swap_recv.at[1], sibling).wait_recv()
    remote(
        cache, kv.at[1 - parity, 1 - core, pl.ds(0, 2048)], swap_send.at[2], swap_recv.at[2], sibling
    ).wait_recv()
    vx[:, :2048, :128] = kv[1, :, :2048]
    here = ((y, z), (z, y))
    diff = lax.broadcasted_iota(jnp.int32, (rows, 256), 1) - lax.rem(
        lax.broadcasted_iota(jnp.int32, (rows, 256), 0), tokens
    )

    def block_of(i):
        c, k = i // 4, lax.rem(i, 4)
        k = jnp.where(c == 0, k, lax.rem(k + 1, 4))
        return c, jnp.where(k == 2, 3, jnp.where(k == 3, 2, k))

    def prepare(i):
        c, slot = block_of(i)

        @pl.when(slot != 0)
        def _():
            remote(qs.at[0, 0], qs.at[slot, c], q_send.at[slot, c], q_recv.at[slot, c], chip(x + 1)).wait_recv()

    def score(i, n, s_ref, top_ref):
        c, slot = block_of(i)
        b, start, size = PIECES[n]
        s = lax.dot_general(
            qs[slot, c], kv[0, b, start : start + size, :], (((1,), (1,)), ((), ())), preferred_element_type=F32
        )
        if size == 256:
            ahead = (2 * wrap(x - slot) + core - 2 * x - b) * ROWS + c * tokens
            s = jnp.where(diff <= ahead, s, NEG)
        s_ref[:, b * 2304 + start : b * 2304 + start + size] = s
        top = s[:, :128]
        for k in range(1, size // 128):
            top = jnp.maximum(top, s[:, k * 128 : (k + 1) * 128])
        top_ref[...] = top if n == 0 else jnp.maximum(top_ref[...], top)

    def weigh(n, s_ref, best):
        b, start, size = PIECES[n]
        p = jnp.exp2(s_ref[:, b * 2304 + start : b * 2304 + start + size] - best)
        o = jnp.dot(p.astype(BF), vx[b, start : start + size, :], preferred_element_type=F32)
        summed[...] = o if n == 0 else summed[...] + o

    wide = lax.broadcasted_iota(jnp.int32, (rows, 128), 1)

    def settle(i, best):
        c, slot = block_of(i)
        ob[slot, c] = summed[:, :128].astype(BF)
        both = jnp.where(wide == 0, best, summed[:, 128:])
        stat[slot, c] = both.T[:8, :]

        @pl.when(slot != 0)
        def _():
            home = chip(x - slot)
            remote(ob.at[slot, c], oin.at[slot, c], o_send.at[slot, c], o_recv.at[slot, c], home).start()
            remote(stat.at[slot, c], stat_in.at[slot, c], t_send.at[slot, c], t_recv.at[slot, c], home).start()

    def finish(c):
        for d in order:
            remote(ob.at[d, c], oin.at[d, c], o_send.at[d, c], o_recv.at[d, c], chip(x + 1)).wait_recv()
            remote(stat.at[d, c], stat_in.at[d, c], t_send.at[d, c], t_recv.at[d, c], chip(x + 1)).wait_recv()
        stats = [stat[0, c], stat_in[1, c], stat_in[2, c], stat_in[3, c]]
        tops = [s[0:1, :] for s in stats]
        peak = jnp.maximum(jnp.maximum(tops[0], tops[1]), jnp.maximum(tops[2], tops[3]))
        factors = [jnp.exp2(t - peak) for t in tops]
        whole = sum(f * s[1:2, :] for f, s in zip(factors, stats))
        inverse = 1.0 / whole
        row = lax.broadcasted_iota(jnp.int32, (128, rows), 0)
        table = jnp.zeros((128, rows), F32)
        for d in range(4):
            table = jnp.where(row == d, factors[d] * inverse, table)
        columns = table.T
        o = ob[0, c].astype(F32) * columns[:, 0:1]
        for d in range(1, 4):
            o = o + oin[d, c].astype(F32) * columns[:, d : d + 1]
        o = o.astype(BF)
        for head in range(4):
            att[:, head * 128 : (head + 1) * 128] = o[head * tokens : (head + 1) * tokens, :]

    def fill(c, half, d):
        a = wrap(here[half][0] + d)

        def step(b, carry):
            t = b * 4 + a if half == 0 else a * 4 + b
            deep = pl.ds(pl.multiple_of(t * 512, 512), 512)
            r = jnp.dot(att[...], w[deep, half * 256 : (half + 1) * 256], preferred_element_type=F32).astype(BF)
            terms[c, half, a, 0, b] = r[:half_rows]
            terms[c, half, a, 1, b] = r[half_rows:]
            return carry

        lax.fori_loop(0, 4, step, 0)

    def copy(c, half, m, src, dst, partner):
        return remote(src, dst, r_send.at[c, half, m], r_recv.at[c, half, m], partner)

    def moves(c, half):
        def block(d, ch):
            return terms.at[c, half, wrap(here[half][0] + d), ch]

        def block2(d, ch):
            return terms2.at[c, half, ch, wrap(here[half][1] + d)]

        ends = (
            (block(2, 0), relay.at[c, half, 0], first(half, 1)),
            (block(2, 1), relay.at[c, half, 1], first(half, -1)),
            (block(1, 1), inbox.at[c, half, 0, 1], first(half, 1)),
            (block(1, 0), inbox.at[c, half, 0, 0], first(half, 1)),
            (block(-1, 0), inbox.at[c, half, 1, 0], first(half, -1)),
            (block(-1, 1), inbox.at[c, half, 1, 1], first(half, -1)),
            (block2(2, 0), relay2.at[c, half, 0], second(half, 1)),
            (block2(2, 1), relay2.at[c, half, 1], second(half, -1)),
            (block2(1, 1), inbox2.at[c, half, 0, 1], second(half, 1)),
            (block2(1, 0), inbox2.at[c, half, 0, 0], second(half, 1)),
            (block2(-1, 0), inbox2.at[c, half, 1, 0], second(half, -1)),
            (block2(-1, 1), inbox2.at[c, half, 1, 1], second(half, -1)),
        )
        return (lambda m: copy(c, half, m, *ends[m])), ends

    def add(dst, src):
        dst[...] = (dst[...].astype(F32) + src[...].astype(F32)).astype(BF)

    def stage0(c):
        finish(c)
        for half in range(2):
            sends, _ = moves(c, half)
            fill(c, half, 2)
            sends(0).start()
            sends(1).start()
        for half in range(2):
            sends, _ = moves(c, half)
            fill(c, half, 1)
            sends(2).start()
            fill(c, half, -1)
            sends(4).start()
        for half in range(2):
            fill(c, half, 0)

    def stage1(c):
        for half in range(2):
            sends, ends = moves(c, half)
            for m, k in ((0, 3), (1, 5)):
                sends(m).wait_recv()
                add(ends[k][0], ends[m][1])
                sends(k).start()

    def stage2(c):
        for half in range(2):
            sends, _ = moves(c, half)
            for m in (2, 4, 3, 5):
                sends(m).wait_recv()

            def merge(b, carry):
                for ch in range(2):
                    got = terms[c, half, here[half][0], ch, b].astype(F32)
                    got = got + inbox[c, half, 0, ch, b].astype(F32) + inbox[c, half, 1, ch, b].astype(F32)
                    terms2[c, half, ch, b] = got.astype(BF)
                return carry

            lax.fori_loop(0, 4, merge, 0)
            for m in (6, 7, 8, 10):
                sends(m).start()

    def stage3(c):
        for half in range(2):
            sends, ends = moves(c, half)
            for m, k in ((6, 9), (7, 11)):
                sends(m).wait_recv()
                add(ends[k][0], ends[m][1])
                sends(k).start()

    def stage4(c):
        for half in range(2):
            sends, _ = moves(c, half)
            for m in (8, 10, 9, 11):
                sends(m).wait_recv()
            for ch in range(2):
                got = terms2[c, half, ch, here[half][1]].astype(F32)
                got = got + inbox2[c, half, 0, ch].astype(F32) + inbox2[c, half, 1, ch].astype(F32)
                start = c * tokens + ch * half_rows
                out[start : start + half_rows, half * 256 : (half + 1) * 256] = got.astype(BF)

    blocks = 4 * parts
    prepare(0)
    for n in range(4):
        score(0, n, sa, top_a)
    keep.wait()
    remote(fresh, kv.at[:, 1 - core, pl.ds(2048, 256)], swap_send.at[4], swap_recv.at[4], sibling).wait_recv()
    vx[:, 2048:, :128] = kv[1, :, 2048:]
    for n in range(4, 6):
        score(0, n, sa, top_a)

    def half_step(i, now, top_now, later, top_later):
        nxt = jnp.minimum(i + 1, blocks - 1)

        @pl.when(i + 1 < blocks)
        def _():
            prepare(nxt)

        best = jnp.max(top_now[...], axis=1, keepdims=True)
        for n in range(6):
            score(nxt, n, later, top_later)
            weigh(n, now, best)
        settle(i, best)

    def fetched(t, carry):
        fetch(t).wait()
        return carry

    def step(p, carry):
        half_step(2 * p, sa, top_a, sb, top_b)

        @pl.when(p == 2)
        def _():
            lax.fori_loop(0, 16, fetched, 0)
            stage0(0)

        @pl.when(p == 3)
        def _():
            stage1(0)

        half_step(2 * p + 1, sb, top_b, sa, top_a)
        return carry

    lax.fori_loop(0, blocks // 2, step, 0)
    stage2(0)
    stage0(1)
    stage3(0)
    stage1(1)
    stage4(0)
    stage2(1)
    stage3(1)
    stage4(1)
    give.wait_send()
    swaps[0].wait_send()
    swaps[1].wait_send()
    passed.wait_send()
    for c in range(parts):
        for d in order:
            query(c, d).wait_send()
            remote(ob.at[d, c], oin.at[d, c], o_send.at[d, c], o_recv.at[d, c], chip(x + 1)).wait_send()
            remote(stat.at[d, c], stat_in.at[d, c], t_send.at[d, c], t_recv.at[d, c], chip(x + 1)).wait_send()
        for half in range(2):
            sends, _ = moves(c, half)
            for m in range(12):
                sends(m).wait_send()

    def drain(half, m, rows):
        message(half, m, chunk(half, 0, 0), rows, sibling).wait_send()

    for half in range(2):
        drain(half, 0, ALL)
        drain(half, 1, ALL)
        drain(half, 2, TOP)
        drain(half, 3, BOTTOM)
        for j in range(4):
            drain(half, 4 + 4 * j, ALL)
            drain(half, 5 + 4 * j, ALL)
            drain(half, 6 + 4 * j, TOP)
            drain(half, 7 + 4 * j, BOTTOM)


def block(hid, gain, wq, wk, wv, cache, w_out, prefix, parts):
    whole = pl.BlockSpec(memory_space=VMEM)
    left = pl.BlockSpec(memory_space=pl.ANY)
    dma = pltpu.SemaphoreType.DMA
    half = np.arange(HEAD_DIM // 2, dtype=np.float64) * 2.0 / HEAD_DIM
    freqs = jnp.asarray(np.tile(500000.0**-half, 2)[None, :], F32)
    rows = 4 * ROWS // parts
    h = rows // 8
    return pl.pallas_call(
        functools.partial(block_kernel, prefix, parts),
        out_shape=jax.ShapeDtypeStruct((ROWS, 512), BF),
        in_specs=[whole] * 3 + [left] * 5,
        out_specs=whole,
        scratch_shapes=[
            pltpu.VMEM((16, ROWS, CUTS[0][1]), BF),
            pltpu.VMEM((16, ROWS, CUTS[1][1]), BF),
            pltpu.VMEM((FEATURES, 512), BF),
            pltpu.VMEM((128, FEATURES), BF),
            pltpu.VMEM((ROWS, 640), F32),
            pltpu.VMEM((ROWS, 128), F32),
            pltpu.VMEM((ROWS, 128), F32),
            pltpu.VMEM((ROWS, 128), F32),
            pltpu.VMEM((ROWS, 128), BF),
            pltpu.VMEM((ROWS, 128), BF),
            pltpu.VMEM((2, ROWS, 128), BF),
            pltpu.VMEM((2, 2, 2304, 128), BF),
            pltpu.VMEM((2, 2304, 256), BF),
            pltpu.VMEM((4, parts, rows, 128), BF),
            pltpu.VMEM((4, parts, rows, 128), BF),
            pltpu.VMEM((4, parts, rows, 128), BF),
            pltpu.VMEM((4, parts, 8, rows), F32),
            pltpu.VMEM((4, parts, 8, rows), F32),
            pltpu.VMEM((rows, 4608), F32),
            pltpu.VMEM((rows, 4608), F32),
            pltpu.VMEM((rows, 128), F32),
            pltpu.VMEM((rows, 128), F32),
            pltpu.VMEM((rows, 256), F32),
            pltpu.VMEM((rows // 4, 512), BF),
            pltpu.VMEM((parts, 2, 4, 2, 4, h, 256), BF),
            pltpu.VMEM((parts, 2, 2, 4, h, 256), BF),
            pltpu.VMEM((parts, 2, 2, 2, 4, h, 256), BF),
            pltpu.VMEM((parts, 2, 2, 4, h, 256), BF),
            pltpu.VMEM((parts, 2, 2, h, 256), BF),
            pltpu.VMEM((parts, 2, 2, 2, h, 256), BF),
            dma((2, 20)),
            dma((2, 20)),
            dma((4,)),
            dma((16,)),
            dma((5,)),
            dma((5,)),
        ]
        + [dma((4, parts))] * 6
        + [dma((parts, 2, 12)), dma((parts, 2, 12))],
        compiler_params=pltpu.CompilerParams(
            collective_id=0, has_side_effects=True, vmem_limit_bytes=62 << 20
        ),
        name="block",
    )(hid, gain, freqs, wq, wk.T, wv.T, cache, w_out)


def body(prefix, parts, hidden_states, norm_gain, w_query, w_key, w_value, cache, w_out):
    gain = norm_gain.reshape(1, FEATURES)
    return block(hidden_states, gain, w_query, w_key, w_value, cache, w_out, prefix, parts)


def solution(mesh):
    in_specs = (P("grp", "tp"), P(), P(None, "tp"), P(None, "tp"), P(None, "tp"), P("grp", "tp"), P("tp", None))
    return jax.shard_map(
        functools.partial(body, 16384, 2),
        mesh=mesh,
        in_specs=in_specs,
        out_specs=P("grp", "tp"),
        check_vma=False,
    )
```

```python
import functools
import math

import jax
import jax.numpy as jnp
import numpy as np
from jax import lax
from jax.experimental import pallas as pl
from jax.experimental.pallas import tpu as pltpu
from jax.sharding import PartitionSpec as P

HEAD_DIM = 128
MESH = pl.DeviceIdType.MESH
BF = jnp.bfloat16
F32 = jnp.float32
ROWS = 256
FEATURES = 8192
CUTS = ((0, 160), (160, 96))
PIECES = ((0, 0, 1024), (0, 1024, 1024), (1, 0, 1024), (1, 1024, 1024), (0, 2048, 256), (1, 2048, 256))
NEG = -1e30
VMEM = pltpu.MemorySpace.VMEM


def place():
    grp = lax.axis_index("grp")
    tp = lax.axis_index("tp")
    return grp // 2, grp % 2, tp // 4, tp % 4


def wrap(i):
    return lax.rem(i + 8, 4)


def greet(partners):
    barrier = pltpu.get_barrier_semaphore()
    for partner in partners:
        pl.semaphore_signal(barrier, inc=1, device_id=partner, device_id_type=MESH)
    pl.semaphore_wait(barrier, len(partners))


def remote(src, dst, send, recv, partner):
    return pltpu.make_async_remote_copy(
        src_ref=src, dst_ref=dst, send_sem=send, recv_sem=recv, device_id=partner, device_id_type=MESH
    )


def block_kernel(
    prefix, parts, hid, gain, freqs, wq_hbm, wk_hbm, wv_hbm, cache, w_hbm,
    out,
    got_a, got_b, w, wkv, acc, squares, cos, sin, part, partner_part, fresh, kv, vx,
    qs, ob, oin, stat, stat_in, sa, sb, top_a, top_b, summed, att,
    terms, relay, inbox, terms2, relay2, inbox2,
    send, recv, load, w_load, swap_send, swap_recv,
    q_send, q_recv, o_send, o_recv, t_send, t_recv, r_send, r_recv,
):
    got = (got_a, got_b)
    tokens = ROWS // parts
    rows = 4 * tokens
    half_rows = tokens // 2
    x, core, z, y = place()
    grp = 2 * x + core
    parity = lax.rem(y, 2)

    def at(dz, dy):
        return wrap(z + dz) * 4 + wrap(y + dy)

    def to(dz, dy):
        return {"grp": grp, "tp": at(dz, dy)}

    def chip(i):
        return {"grp": 2 * wrap(i) + core, "tp": z * 4 + y}

    def chunk(half, a, b):
        return at(b, a) if half == 0 else at(a, b)

    def first(half, d):
        return to(0, d) if half == 0 else to(d, 0)

    def second(half, d):
        return to(d, 0) if half == 0 else to(0, d)

    partner = {"grp": grp, "tp": z * 4 + y + 1 - 2 * parity}
    sibling = {"grp": grp + 1 - 2 * core, "tp": z * 4 + y}
    loads = [
        pltpu.make_async_copy(wq_hbm, w, load.at[0]),
        pltpu.make_async_copy(wk_hbm, wkv.at[pl.ds(0, 64)], load.at[1]),
        pltpu.make_async_copy(wv_hbm, wkv.at[pl.ds(64, 64)], load.at[2]),
    ]
    for one in loads:
        one.start()
    own_cache = pltpu.make_async_copy(cache, kv.at[parity, core, pl.ds(0, 2048)], load.at[3])
    own_cache.start()
    for half, (start, size) in enumerate(CUTS):
        got[half][at(0, 0)] = hid[start : start + size, :]
    order = (1, 3, 2)
    greet([to(0, 1), to(0, -1), to(1, 0), to(-1, 0), sibling, chip(x + 1), chip(x + 2), chip(x + 3)])

    TOP, BOTTOM, ALL = 0, 1, 2
    on = jnp.where(parity == 0, -1, 1)
    passes, takes = 3 - parity, 2 + parity

    def message(half, m, idx, which, partner):
        size = CUTS[half][1]
        ref = got[half].at[idx, pl.ds(which % 2 * size // 2, size if which == ALL else size // 2)]
        return remote(ref, ref, send.at[half, m], recv.at[half, m], partner)

    for m, d in ((0, 1), (1, -1)):
        for half in range(2):
            message(half, m, chunk(half, 0, 0), ALL, first(half, d)).start()
    for m, d in ((4, 1), (5, -1)):
        for half in range(2):
            message(half, m, chunk(half, 0, 0), ALL, second(half, d)).start()
    acc[...] = jnp.zeros_like(acc)
    vx[:, :, 128:] = jnp.ones((2, 2304, 128), BF)
    squares[...] = jnp.zeros_like(squares)

    def absorb(half, t):
        start, size = CUTS[half]
        here = slice(start, start + size)
        h = got[half][t].astype(F32)
        sq = h * h
        squares[here] += sq[:, :128] + sq[:, 128:256] + sq[:, 256:384] + sq[:, 384:]
        depth = pl.ds(pl.multiple_of(t * 512, 512), 512)
        scaled = (h * gain[:, depth]).astype(BF)
        acc[here, :512] += jnp.dot(scaled, w[depth, :], preferred_element_type=F32)
        acc[here, 512:] += lax.dot_general(
            scaled, wkv[:, depth], (((1,), (1,)), ((), ())), preferred_element_type=F32
        )

    def absorb_all(count, place_of):
        def step(i, carry):
            for half in range(2):
                absorb(half, chunk(half, *place_of(i)))
            return carry

        lax.fori_loop(0, count, step, 0)

    def arrived(half, m, idx, rows):
        message(half, m, idx, rows, sibling).wait_recv()

    def spread(half, j, idx):
        message(half, 4 + 4 * j, idx, ALL, second(half, 1)).start()
        message(half, 5 + 4 * j, idx, ALL, second(half, -1)).start()

    lane = lax.broadcasted_iota(jnp.int32, (ROWS, 128), 1)
    row = lax.broadcasted_iota(jnp.int32, (ROWS, 128), 0)
    angles = (row + (prefix + grp * ROWS)).astype(F32) * freqs[...]
    cos[...] = jnp.cos(angles)
    sine = jnp.sin(angles)
    sin[...] = jnp.where(lane < 64, -sine, sine)
    for one in loads:
        one.wait()
    absorb_all(1, lambda i: (0, 0))
    for half in range(2):
        idx = chunk(half, -1, 0)
        arrived(half, 0, idx, ALL)
        if half == 1:
            message(half, 2, idx, TOP, first(half, 1)).start()
        spread(half, 1, idx)
    for half in range(2):
        idx = chunk(half, 1, 0)
        arrived(half, 1, idx, ALL)
        if half == 1:
            message(half, 3, idx, BOTTOM, first(half, -1)).start()
        else:
            message(half, passes, chunk(half, -on, 0), ALL, first(half, on)).start()
        spread(half, 2, idx)
    mine = kv.at[parity, core, pl.ds(0, 2048)]
    swaps = [
        remote(cache, mine, swap_send.at[0], swap_recv.at[0], partner),
        remote(cache, mine, swap_send.at[1], swap_recv.at[1], sibling),
    ]
    for one in swaps:
        one.start()
    absorb_all(2, lambda i: (2 * i - 1, 0))

    def neighbours(j, a):
        for half in range(2):
            idx = chunk(half, a, -1)
            arrived(half, 4 + 4 * j, idx, ALL)
            if half == 0:
                message(half, 6 + 4 * j, idx, TOP, second(half, 1)).start()
            idx = chunk(half, a, 1)
            arrived(half, 5 + 4 * j, idx, ALL)
            if half == 0:
                message(half, 7 + 4 * j, idx, BOTTOM, second(half, -1)).start()
            else:
                message(half, 4 + passes + 4 * j, chunk(half, a, -on), ALL, second(half, on)).start()
        absorb_all(2, lambda i: (a, 2 * i - 1))

    def opposite(j, a):
        for half in range(2):
            idx = chunk(half, a, 2)
            if half == 0:
                arrived(half, 6 + 4 * j, idx, TOP)
                arrived(half, 7 + 4 * j, idx, BOTTOM)
            else:
                arrived(half, 4 + takes + 4 * j, idx, ALL)
        absorb_all(1, lambda i: (a, 2))

    neighbours(0, 0)
    for half in range(2):
        idx = chunk(half, 2, 0)
        if half == 1:
            arrived(half, 2, idx, TOP)
            arrived(half, 3, idx, BOTTOM)
        else:
            arrived(half, takes, idx, ALL)
        spread(half, 3, idx)
    absorb_all(1, lambda i: (2, 0))

    def sweep(j, carry):
        neighbours(j, jnp.where(j == 1, -1, j - 1))
        return carry

    lax.fori_loop(1, 4, sweep, 0)
    theirs = kv.at[1 - parity, core, pl.ds(0, 2048)]
    remote(cache, theirs, swap_send.at[0], swap_recv.at[0], partner).wait_recv()
    passed = remote(theirs, theirs, swap_send.at[2], swap_recv.at[2], sibling)
    passed.start()

    def sweep_far(j, carry):
        opposite(j, jnp.where(j == 0, 0, jnp.where(j == 1, -1, j - 1)))
        return carry

    lax.fori_loop(0, 4, sweep_far, 0)

    mean = jnp.sum(squares[...], axis=1, keepdims=True) * (1.0 / FEATURES)
    root = lax.rsqrt(mean + 1e-05)
    own = acc[:, 512:] * root
    part[...] = own.astype(BF)
    swap = remote(part, partner_part, swap_send.at[3], swap_recv.at[3], partner)
    swap.start()
    def rope(v):
        return v * cos[...] + pltpu.roll(v, 64, 1) * sin[...]

    scale = math.log2(math.e) / math.sqrt(HEAD_DIM)
    for head in range(4):
        turned = (rope(acc[:, head * 128 : (head + 1) * 128] * root) * scale).astype(BF)
        for i in range(parts):
            qs[0, i, head * tokens : (head + 1) * tokens, :] = turned[i * tokens : (i + 1) * tokens, :]

    def query(c, d):
        return remote(qs.at[0, c], qs.at[d, c], q_send.at[d, c], q_recv.at[d, c], chip(x + d))

    for c in range(parts):
        for d in order:
            query(c, d).start()

    def fetch(t):
        spot = w.at[pl.ds(pl.multiple_of(t * 512, 512), 512)]
        return pltpu.make_async_copy(w_hbm.at[:, pl.ds(pl.multiple_of(t * 512, 512), 512)], spot, w_load.at[t])

    def begin(t, carry):
        fetch(t).start()
        return carry

    lax.fori_loop(0, 16, begin, 0)
    swap.wait()
    other = partner_part[...].astype(F32)
    left = jnp.where(parity == 0, own, other)
    right = jnp.where(parity == 0, other, own)
    key = jnp.where(lane < 64, left, pltpu.roll(right, 64, 1))
    value = jnp.where(lane < 64, pltpu.roll(left, 64, 1), right)
    fresh[0] = rope(key).astype(BF)
    fresh[1] = value.astype(BF)
    spot = kv.at[:, core, pl.ds(2048, 256)]
    keep = pltpu.make_async_copy(fresh, spot, load.at[0])
    keep.start()
    give = remote(fresh, spot, swap_send.at[4], swap_recv.at[4], sibling)
    give.start()
    own_cache.wait()
    remote(cache, kv.at[parity, 1 - core, pl.ds(0, 2048)], swap_send.at[1], swap_recv.at[1], sibling).wait_recv()
    remote(
        cache, kv.at[1 - parity, 1 - core, pl.ds(0, 2048)], swap_send.at[2], swap_recv.at[2], sibling
    ).wait_recv()
    vx[:, :2048, :128] = kv[1, :, :2048]
    here = ((y, z), (z, y))
    diff = lax.broadcasted_iota(jnp.int32, (rows, 256), 1) - lax.rem(
        lax.broadcasted_iota(jnp.int32, (rows, 256), 0), tokens
    )

    def block_of(i):
        c, k = i // 4, lax.rem(i, 4)
        k = jnp.where(c == 0, k, lax.rem(k + 1, 4))
        return c, jnp.where(k == 2, 3, jnp.where(k == 3, 2, k))

    def prepare(i):
        c, slot = block_of(i)

        @pl.when(slot != 0)
        def _():
            remote(qs.at[0, 0], qs.at[slot, c], q_send.at[slot, c], q_recv.at[slot, c], chip(x + 1)).wait_recv()

    def score(i, n, s_ref, top_ref):
        c, slot = block_of(i)
        b, start, size = PIECES[n]
        s = lax.dot_general(
            qs[slot, c], kv[0, b, start : start + size, :], (((1,), (1,)), ((), ())), preferred_element_type=F32
        )
        if size == 256:
            ahead = (2 * wrap(x - slot) + core - 2 * x - b) * ROWS + c * tokens
            s = jnp.where(diff <= ahead, s, NEG)
        s_ref[:, b * 2304 + start : b * 2304 + start + size] = s
        top = s[:, :128]
        for k in range(1, size // 128):
            top = jnp.maximum(top, s[:, k * 128 : (k + 1) * 128])
        top_ref[...] = top if n == 0 else jnp.maximum(top_ref[...], top)

    def weigh(n, s_ref, best):
        b, start, size = PIECES[n]
        p = jnp.exp2(s_ref[:, b * 2304 + start : b * 2304 + start + size] - best)
        o = jnp.dot(p.astype(BF), vx[b, start : start + size, :], preferred_element_type=F32)
        summed[...] = o if n == 0 else summed[...] + o

    wide = lax.broadcasted_iota(jnp.int32, (rows, 128), 1)

    def settle(i, best):
        c, slot = block_of(i)
        ob[slot, c] = summed[:, :128].astype(BF)
        both = jnp.where(wide == 0, best, summed[:, 128:])
        stat[slot, c] = both.T[:8, :]

        @pl.when(slot != 0)
        def _():
            home = chip(x - slot)
            remote(ob.at[slot, c], oin.at[slot, c], o_send.at[slot, c], o_recv.at[slot, c], home).start()
            remote(stat.at[slot, c], stat_in.at[slot, c], t_send.at[slot, c], t_recv.at[slot, c], home).start()

    def finish(c):
        for d in order:
            remote(ob.at[d, c], oin.at[d, c], o_send.at[d, c], o_recv.at[d, c], chip(x + 1)).wait_recv()
            remote(stat.at[d, c], stat_in.at[d, c], t_send.at[d, c], t_recv.at[d, c], chip(x + 1)).wait_recv()
        stats = [stat[0, c], stat_in[1, c], stat_in[2, c], stat_in[3, c]]
        tops = [s[0:1, :] for s in stats]
        peak = jnp.maximum(jnp.maximum(tops[0], tops[1]), jnp.maximum(tops[2], tops[3]))
        factors = [jnp.exp2(t - peak) for t in tops]
        whole = sum(f * s[1:2, :] for f, s in zip(factors, stats))
        inverse = 1.0 / whole
        row = lax.broadcasted_iota(jnp.int32, (128, rows), 0)
        table = jnp.zeros((128, rows), F32)
        for d in range(4):
            table = jnp.where(row == d, factors[d] * inverse, table)
        columns = table.T
        o = ob[0, c].astype(F32) * columns[:, 0:1]
        for d in range(1, 4):
            o = o + oin[d, c].astype(F32) * columns[:, d : d + 1]
        o = o.astype(BF)
        for head in range(4):
            att[:, head * 128 : (head + 1) * 128] = o[head * tokens : (head + 1) * tokens, :]

    def fill(c, half, d):
        a = wrap(here[half][0] + d)

        def step(b, carry):
            t = b * 4 + a if half == 0 else a * 4 + b
            deep = pl.ds(pl.multiple_of(t * 512, 512), 512)
            r = jnp.dot(att[...], w[deep, half * 256 : (half + 1) * 256], preferred_element_type=F32).astype(BF)
            terms[c, half, a, 0, b] = r[:half_rows]
            terms[c, half, a, 1, b] = r[half_rows:]
            return carry

        lax.fori_loop(0, 4, step, 0, unroll=True)

    def copy(c, half, m, src, dst, partner):
        return remote(src, dst, r_send.at[c, half, m], r_recv.at[c, half, m], partner)

    def moves(c, half):
        def block(d, ch):
            return terms.at[c, half, wrap(here[half][0] + d), ch]

        def block2(d, ch):
            return terms2.at[c, half, ch, wrap(here[half][1] + d)]

        ends = (
            (block(2, 0), relay.at[c, half, 0], first(half, 1)),
            (block(2, 1), relay.at[c, half, 1], first(half, -1)),
            (block(1, 1), inbox.at[c, half, 0, 1], first(half, 1)),
            (block(1, 0), inbox.at[c, half, 0, 0], first(half, 1)),
            (block(-1, 0), inbox.at[c, half, 1, 0], first(half, -1)),
            (block(-1, 1), inbox.at[c, half, 1, 1], first(half, -1)),
            (block2(2, 0), relay2.at[c, half, 0], second(half, 1)),
            (block2(2, 1), relay2.at[c, half, 1], second(half, -1)),
            (block2(1, 1), inbox2.at[c, half, 0, 1], second(half, 1)),
            (block2(1, 0), inbox2.at[c, half, 0, 0], second(half, 1)),
            (block2(-1, 0), inbox2.at[c, half, 1, 0], second(half, -1)),
            (block2(-1, 1), inbox2.at[c, half, 1, 1], second(half, -1)),
        )
        return (lambda m: copy(c, half, m, *ends[m])), ends

    def add(dst, src):
        dst[...] = (dst[...].astype(F32) + src[...].astype(F32)).astype(BF)

    def stage0(c):
        finish(c)
        for half in range(2):
            sends, _ = moves(c, half)
            fill(c, half, 2)
            sends(0).start()
            sends(1).start()
        for half in range(2):
            sends, _ = moves(c, half)
            fill(c, half, 1)
            sends(2).start()
            fill(c, half, -1)
            sends(4).start()
        for half in range(2):
            fill(c, half, 0)

    def stage1(c):
        for half in range(2):
            sends, ends = moves(c, half)
            for m, k in ((0, 3), (1, 5)):
                sends(m).wait_recv()
                add(ends[k][0], ends[m][1])
                sends(k).start()

    def stage2(c):
        for half in range(2):
            sends, _ = moves(c, half)
            for m in (2, 4, 3, 5):
                sends(m).wait_recv()

            def merge(b, carry):
                for ch in range(2):
                    got = terms[c, half, here[half][0], ch, b].astype(F32)
                    got = got + inbox[c, half, 0, ch, b].astype(F32) + inbox[c, half, 1, ch, b].astype(F32)
                    terms2[c, half, ch, b] = got.astype(BF)
                return carry

            lax.fori_loop(0, 4, merge, 0, unroll=True)
            for m in (6, 7, 8, 10):
                sends(m).start()

    def stage3(c):
        for half in range(2):
            sends, ends = moves(c, half)
            for m, k in ((6, 9), (7, 11)):
                sends(m).wait_recv()
                add(ends[k][0], ends[m][1])
                sends(k).start()

    def stage4(c):
        for half in range(2):
            sends, _ = moves(c, half)
            for m in (8, 10, 9, 11):
                sends(m).wait_recv()
            for ch in range(2):
                got = terms2[c, half, ch, here[half][1]].astype(F32)
                got = got + inbox2[c, half, 0, ch].astype(F32) + inbox2[c, half, 1, ch].astype(F32)
                start = c * tokens + ch * half_rows
                out[start : start + half_rows, half * 256 : (half + 1) * 256] = got.astype(BF)

    blocks = 4 * parts
    prepare(0)
    for n in range(4):
        score(0, n, sa, top_a)
    keep.wait()
    remote(fresh, kv.at[:, 1 - core, pl.ds(2048, 256)], swap_send.at[4], swap_recv.at[4], sibling).wait_recv()
    vx[:, 2048:, :128] = kv[1, :, 2048:]
    for n in range(4, 6):
        score(0, n, sa, top_a)

    def half_step(i, now, top_now, later, top_later):
        nxt = jnp.minimum(i + 1, blocks - 1)

        @pl.when(i + 1 < blocks)
        def _():
            prepare(nxt)

        best = jnp.max(top_now[...], axis=1, keepdims=True)
        for n in range(6):
            score(nxt, n, later, top_later)
            weigh(n, now, best)
        settle(i, best)

    def fetched(t, carry):
        fetch(t).wait()
        return carry

    def step(p, carry):
        half_step(2 * p, sa, top_a, sb, top_b)

        @pl.when(p == 2)
        def _():
            lax.fori_loop(0, 16, fetched, 0)
            stage0(0)

        @pl.when(p == 3)
        def _():
            stage1(0)

        half_step(2 * p + 1, sb, top_b, sa, top_a)
        return carry

    lax.fori_loop(0, blocks // 2, step, 0)
    stage2(0)
    stage0(1)
    stage3(0)
    stage1(1)
    stage4(0)
    stage2(1)
    stage3(1)
    stage4(1)
    give.wait_send()
    swaps[0].wait_send()
    swaps[1].wait_send()
    passed.wait_send()
    for c in range(parts):
        for d in order:
            query(c, d).wait_send()
            remote(ob.at[d, c], oin.at[d, c], o_send.at[d, c], o_recv.at[d, c], chip(x + 1)).wait_send()
            remote(stat.at[d, c], stat_in.at[d, c], t_send.at[d, c], t_recv.at[d, c], chip(x + 1)).wait_send()
        for half in range(2):
            sends, _ = moves(c, half)
            for m in range(12):
                sends(m).wait_send()

    def drain(half, m, rows):
        message(half, m, chunk(half, 0, 0), rows, sibling).wait_send()

    for half in range(2):
        drain(half, 0, ALL)
        drain(half, 1, ALL)
        if half == 1:
            drain(half, 2, TOP)
            drain(half, 3, BOTTOM)
        else:
            drain(half, passes, ALL)
        for j in range(4):
            drain(half, 4 + 4 * j, ALL)
            drain(half, 5 + 4 * j, ALL)
            if half == 0:
                drain(half, 6 + 4 * j, TOP)
                drain(half, 7 + 4 * j, BOTTOM)
            else:
                drain(half, 4 + passes + 4 * j, ALL)


def block(hid, gain, wq, wk, wv, cache, w_out, prefix, parts):
    whole = pl.BlockSpec(memory_space=VMEM)
    left = pl.BlockSpec(memory_space=pl.ANY)
    dma = pltpu.SemaphoreType.DMA
    half = np.arange(HEAD_DIM // 2, dtype=np.float64) * 2.0 / HEAD_DIM
    freqs = jnp.asarray(np.tile(500000.0**-half, 2)[None, :], F32)
    rows = 4 * ROWS // parts
    h = rows // 8
    return pl.pallas_call(
        functools.partial(block_kernel, prefix, parts),
        out_shape=jax.ShapeDtypeStruct((ROWS, 512), BF),
        in_specs=[whole] * 3 + [left] * 5,
        out_specs=whole,
        scratch_shapes=[
            pltpu.VMEM((16, CUTS[0][1], 512), BF),
            pltpu.VMEM((16, CUTS[1][1], 512), BF),
            pltpu.VMEM((FEATURES, 512), BF),
            pltpu.VMEM((128, FEATURES), BF),
            pltpu.VMEM((ROWS, 640), F32),
            pltpu.VMEM((ROWS, 128), F32),
            pltpu.VMEM((ROWS, 128), F32),
            pltpu.VMEM((ROWS, 128), F32),
            pltpu.VMEM((ROWS, 128), BF),
            pltpu.VMEM((ROWS, 128), BF),
            pltpu.VMEM((2, ROWS, 128), BF),
            pltpu.VMEM((2, 2, 2304, 128), BF),
            pltpu.VMEM((2, 2304, 256), BF),
            pltpu.VMEM((4, parts, rows, 128), BF),
            pltpu.VMEM((4, parts, rows, 128), BF),
            pltpu.VMEM((4, parts, rows, 128), BF),
            pltpu.VMEM((4, parts, 8, rows), F32),
            pltpu.VMEM((4, parts, 8, rows), F32),
            pltpu.VMEM((rows, 4608), F32),
            pltpu.VMEM((rows, 4608), F32),
            pltpu.VMEM((rows, 128), F32),
            pltpu.VMEM((rows, 128), F32),
            pltpu.VMEM((rows, 256), F32),
            pltpu.VMEM((rows // 4, 512), BF),
            pltpu.VMEM((parts, 2, 4, 2, 4, h, 256), BF),
            pltpu.VMEM((parts, 2, 2, 4, h, 256), BF),
            pltpu.VMEM((parts, 2, 2, 2, 4, h, 256), BF),
            pltpu.VMEM((parts, 2, 2, 4, h, 256), BF),
            pltpu.VMEM((parts, 2, 2, h, 256), BF),
            pltpu.VMEM((parts, 2, 2, 2, h, 256), BF),
            dma((2, 20)),
            dma((2, 20)),
            dma((4,)),
            dma((16,)),
            dma((5,)),
            dma((5,)),
        ]
        + [dma((4, parts))] * 6
        + [dma((parts, 2, 12)), dma((parts, 2, 12))],
        compiler_params=pltpu.CompilerParams(
            collective_id=0, has_side_effects=True, vmem_limit_bytes=62 << 20
        ),
        name="block",
    )(hid, gain, freqs, wq, wk.T, wv.T, cache, w_out)


def body(prefix, parts, hidden_states, norm_gain, w_query, w_key, w_value, cache, w_out):
    gain = norm_gain.reshape(1, FEATURES)
    return block(hidden_states, gain, w_query, w_key, w_value, cache, w_out, prefix, parts)


def solution(mesh):
    in_specs = (P("grp", "tp"), P(), P(None, "tp"), P(None, "tp"), P(None, "tp"), P("grp", "tp"), P("tp", None))
    return jax.shard_map(
        functools.partial(body, 16384, 2),
        mesh=mesh,
        in_specs=in_specs,
        out_specs=P("grp", "tp"),
        check_vma=False,
    )
```

```python
import functools
import math

import jax
import jax.numpy as jnp
import numpy as np
from jax import lax
from jax.experimental import pallas as pl
from jax.experimental.pallas import tpu as pltpu
from jax.sharding import PartitionSpec as P

HEAD_DIM = 128
MESH = pl.DeviceIdType.MESH
BF = jnp.bfloat16
F32 = jnp.float32
ROWS = 256
FEATURES = 8192
CUTS = ((0, 160), (160, 96))
PIECES = ((0, 0, 1024), (0, 1024, 1024), (1, 0, 1024), (1, 1024, 1024), (0, 2048, 256), (1, 2048, 256))
NEG = -1e30
VMEM = pltpu.MemorySpace.VMEM


def place():
    grp = lax.axis_index("grp")
    tp = lax.axis_index("tp")
    return grp // 2, grp % 2, tp // 4, tp % 4


def wrap(i):
    return lax.rem(i + 8, 4)


def greet(partners):
    barrier = pltpu.get_barrier_semaphore()
    for partner in partners:
        pl.semaphore_signal(barrier, inc=1, device_id=partner, device_id_type=MESH)
    pl.semaphore_wait(barrier, len(partners))


def remote(src, dst, send, recv, partner):
    return pltpu.make_async_remote_copy(
        src_ref=src, dst_ref=dst, send_sem=send, recv_sem=recv, device_id=partner, device_id_type=MESH
    )


def block_kernel(
    prefix, parts, hid, gain, freqs, wq_hbm, wk_hbm, wv_hbm, cache, w_hbm,
    out,
    got_a, got_b, w, wkv, acc, squares, cos, sin, part, partner_part, fresh, kv, vx,
    qs, ob, oin, stat, stat_in, sa, sb, top_a, top_b, summed, att,
    terms, relay, inbox, terms2, relay2, inbox2,
    send, recv, load, w_load, swap_send, swap_recv,
    q_send, q_recv, o_send, o_recv, t_send, t_recv, r_send, r_recv,
):
    got = (got_a, got_b)
    tokens = ROWS // parts
    rows = 4 * tokens
    half_rows = tokens // 2
    x, core, z, y = place()
    grp = 2 * x + core
    parity = lax.rem(y, 2)

    def at(dz, dy):
        return wrap(z + dz) * 4 + wrap(y + dy)

    def to(dz, dy):
        return {"grp": grp, "tp": at(dz, dy)}

    def chip(i):
        return {"grp": 2 * wrap(i) + core, "tp": z * 4 + y}

    def chunk(half, a, b):
        return at(b, a) if half == 0 else at(a, b)

    def first(half, d):
        return to(0, d) if half == 0 else to(d, 0)

    def second(half, d):
        return to(d, 0) if half == 0 else to(0, d)

    partner = {"grp": grp, "tp": z * 4 + y + 1 - 2 * parity}
    sibling = {"grp": grp + 1 - 2 * core, "tp": z * 4 + y}
    loads = [
        pltpu.make_async_copy(wq_hbm, w, load.at[0]),
        pltpu.make_async_copy(wk_hbm, wkv.at[pl.ds(0, 64)], load.at[1]),
        pltpu.make_async_copy(wv_hbm, wkv.at[pl.ds(64, 64)], load.at[2]),
    ]
    for one in loads:
        one.start()
    own_cache = pltpu.make_async_copy(cache, kv.at[parity, core, pl.ds(0, 2048)], load.at[3])
    own_cache.start()
    for half, (start, size) in enumerate(CUTS):
        got[half][at(0, 0)] = hid[start : start + size, :]
    order = (3, 2, 1)
    greet([to(0, 1), to(0, -1), to(1, 0), to(-1, 0), sibling, chip(x + 1), chip(x + 2), chip(x + 3)])

    TOP, BOTTOM, ALL = 0, 1, 2
    on = jnp.where(parity == 0, -1, 1)
    passes, takes = 3 - parity, 2 + parity

    def message(half, m, idx, which, partner):
        size = CUTS[half][1]
        ref = got[half].at[idx, pl.ds(which % 2 * size // 2, size if which == ALL else size // 2)]
        return remote(ref, ref, send.at[half, m], recv.at[half, m], partner)

    for m, d in ((0, 1), (1, -1)):
        for half in range(2):
            message(half, m, chunk(half, 0, 0), ALL, first(half, d)).start()
    for m, d in ((4, 1), (5, -1)):
        for half in range(2):
            message(half, m, chunk(half, 0, 0), ALL, second(half, d)).start()
    acc[...] = jnp.zeros_like(acc)
    vx[:, :, 128:] = jnp.ones((2, 2304, 128), BF)
    squares[...] = jnp.zeros_like(squares)

    def absorb(half, t):
        start, size = CUTS[half]
        here = slice(start, start + size)
        h = got[half][t].astype(F32)
        sq = h * h
        squares[here] += sq[:, :128] + sq[:, 128:256] + sq[:, 256:384] + sq[:, 384:]
        depth = pl.ds(pl.multiple_of(t * 512, 512), 512)
        scaled = (h * gain[:, depth]).astype(BF)
        acc[here, :512] += jnp.dot(scaled, w[depth, :], preferred_element_type=F32)
        acc[here, 512:] += lax.dot_general(
            scaled, wkv[:, depth], (((1,), (1,)), ((), ())), preferred_element_type=F32
        )

    def absorb_all(count, place_of):
        def step(i, carry):
            for half in range(2):
                absorb(half, chunk(half, *place_of(i)))
            return carry

        lax.fori_loop(0, count, step, 0)

    def arrived(half, m, idx, rows):
        message(half, m, idx, rows, sibling).wait_recv()

    def spread(half, j, idx):
        message(half, 4 + 4 * j, idx, ALL, second(half, 1)).start()
        message(half, 5 + 4 * j, idx, ALL, second(half, -1)).start()

    lane = lax.broadcasted_iota(jnp.int32, (ROWS, 128), 1)
    row = lax.broadcasted_iota(jnp.int32, (ROWS, 128), 0)
    angles = (row + (prefix + grp * ROWS)).astype(F32) * freqs[...]
    cos[...] = jnp.cos(angles)
    sine = jnp.sin(angles)
    sin[...] = jnp.where(lane < 64, -sine, sine)
    for one in loads:
        one.wait()
    absorb_all(1, lambda i: (0, 0))
    for half in range(2):
        idx = chunk(half, -1, 0)
        arrived(half, 0, idx, ALL)
        if half == 1:
            message(half, 2, idx, TOP, first(half, 1)).start()
        spread(half, 1, idx)
    for half in range(2):
        idx = chunk(half, 1, 0)
        arrived(half, 1, idx, ALL)
        if half == 1:
            message(half, 3, idx, BOTTOM, first(half, -1)).start()
        else:
            message(half, passes, chunk(half, -on, 0), ALL, first(half, on)).start()
        spread(half, 2, idx)
    mine = kv.at[parity, core, pl.ds(0, 2048)]
    swaps = [
        remote(cache, mine, swap_send.at[0], swap_recv.at[0], partner),
        remote(cache, mine, swap_send.at[1], swap_recv.at[1], sibling),
    ]
    for one in swaps:
        one.start()
    absorb_all(2, lambda i: (2 * i - 1, 0))

    def neighbours(j, a):
        for half in range(2):
            idx = chunk(half, a, -1)
            arrived(half, 4 + 4 * j, idx, ALL)
            if half == 0:
                message(half, 6 + 4 * j, idx, TOP, second(half, 1)).start()
            idx = chunk(half, a, 1)
            arrived(half, 5 + 4 * j, idx, ALL)
            if half == 0:
                message(half, 7 + 4 * j, idx, BOTTOM, second(half, -1)).start()
            else:
                message(half, 4 + passes + 4 * j, chunk(half, a, -on), ALL, second(half, on)).start()
        absorb_all(2, lambda i: (a, 2 * i - 1))

    def opposite(j, a):
        for half in range(2):
            idx = chunk(half, a, 2)
            if half == 0:
                arrived(half, 6 + 4 * j, idx, TOP)
                arrived(half, 7 + 4 * j, idx, BOTTOM)
            else:
                arrived(half, 4 + takes + 4 * j, idx, ALL)
        absorb_all(1, lambda i: (a, 2))

    neighbours(0, 0)
    for half in range(2):
        idx = chunk(half, 2, 0)
        if half == 1:
            arrived(half, 2, idx, TOP)
            arrived(half, 3, idx, BOTTOM)
        else:
            arrived(half, takes, idx, ALL)
        spread(half, 3, idx)
    absorb_all(1, lambda i: (2, 0))

    def sweep(j, carry):
        neighbours(j, jnp.where(j == 1, -1, j - 1))
        return carry

    lax.fori_loop(1, 4, sweep, 0)
    theirs = kv.at[1 - parity, core, pl.ds(0, 2048)]
    remote(cache, theirs, swap_send.at[0], swap_recv.at[0], partner).wait_recv()
    passed = remote(theirs, theirs, swap_send.at[2], swap_recv.at[2], sibling)
    passed.start()

    def sweep_far(j, carry):
        opposite(j, jnp.where(j == 0, 0, jnp.where(j == 1, -1, j - 1)))
        return carry

    lax.fori_loop(0, 4, sweep_far, 0)

    mean = jnp.sum(squares[...], axis=1, keepdims=True) * (1.0 / FEATURES)
    root = lax.rsqrt(mean + 1e-05)
    own = acc[:, 512:] * root
    part[...] = own.astype(BF)
    swap = remote(part, partner_part, swap_send.at[3], swap_recv.at[3], partner)
    swap.start()
    def rope(v):
        return v * cos[...] + pltpu.roll(v, 64, 1) * sin[...]

    scale = math.log2(math.e) / math.sqrt(HEAD_DIM)
    for head in range(4):
        turned = (rope(acc[:, head * 128 : (head + 1) * 128] * root) * scale).astype(BF)
        for i in range(parts):
            qs[0, i, head * tokens : (head + 1) * tokens, :] = turned[i * tokens : (i + 1) * tokens, :]

    def query(c, d):
        return remote(qs.at[0, c], qs.at[d, c], q_send.at[d, c], q_recv.at[d, c], chip(x + d))

    for c in range(parts):
        for d in order:
            query(c, d).start()

    def fetch(t):
        spot = w.at[pl.ds(pl.multiple_of(t * 512, 512), 512)]
        return pltpu.make_async_copy(w_hbm.at[:, pl.ds(pl.multiple_of(t * 512, 512), 512)], spot, w_load.at[t])

    def begin(t, carry):
        fetch(t).start()
        return carry

    lax.fori_loop(0, 16, begin, 0)
    swap.wait()
    other = partner_part[...].astype(F32)
    left = jnp.where(parity == 0, own, other)
    right = jnp.where(parity == 0, other, own)
    key = jnp.where(lane < 64, left, pltpu.roll(right, 64, 1))
    value = jnp.where(lane < 64, pltpu.roll(left, 64, 1), right)
    fresh[0] = rope(key).astype(BF)
    fresh[1] = value.astype(BF)
    spot = kv.at[:, core, pl.ds(2048, 256)]
    keep = pltpu.make_async_copy(fresh, spot, load.at[0])
    keep.start()
    give = remote(fresh, spot, swap_send.at[4], swap_recv.at[4], sibling)
    give.start()
    own_cache.wait()
    remote(cache, kv.at[parity, 1 - core, pl.ds(0, 2048)], swap_send.at[1], swap_recv.at[1], sibling).wait_recv()
    remote(
        cache, kv.at[1 - parity, 1 - core, pl.ds(0, 2048)], swap_send.at[2], swap_recv.at[2], sibling
    ).wait_recv()
    vx[:, :2048, :128] = kv[1, :, :2048]
    here = ((y, z), (z, y))
    diff = lax.broadcasted_iota(jnp.int32, (rows, 256), 1) - lax.rem(
        lax.broadcasted_iota(jnp.int32, (rows, 256), 0), tokens
    )

    def block_of(i):
        c, k = i // 4, lax.rem(i, 4)
        k = jnp.where(c == 0, k, lax.rem(k + 1, 4))
        return c, jnp.where(k == 0, 0, 4 - k)

    def prepare(i):
        c, slot = block_of(i)

        @pl.when(slot != 0)
        def _():
            remote(qs.at[0, 0], qs.at[slot, c], q_send.at[slot, c], q_recv.at[slot, c], chip(x + 1)).wait_recv()

    def score(i, n, s_ref, top_ref):
        c, slot = block_of(i)
        b, start, size = PIECES[n]
        s = lax.dot_general(
            qs[slot, c], kv[0, b, start : start + size, :], (((1,), (1,)), ((), ())), preferred_element_type=F32
        )
        if size == 256:
            ahead = (2 * wrap(x - slot) + core - 2 * x - b) * ROWS + c * tokens
            s = jnp.where(diff <= ahead, s, NEG)
        s_ref[:, b * 2304 + start : b * 2304 + start + size] = s
        top = s[:, :128]
        for k in range(1, size // 128):
            top = jnp.maximum(top, s[:, k * 128 : (k + 1) * 128])
        top_ref[...] = top if n == 0 else jnp.maximum(top_ref[...], top)

    def weigh(n, s_ref, best):
        b, start, size = PIECES[n]
        p = jnp.exp2(s_ref[:, b * 2304 + start : b * 2304 + start + size] - best)
        o = jnp.dot(p.astype(BF), vx[b, start : start + size, :], preferred_element_type=F32)
        summed[...] = o if n == 0 else summed[...] + o

    wide = lax.broadcasted_iota(jnp.int32, (rows, 128), 1)

    def settle(i, best):
        c, slot = block_of(i)
        ob[slot, c] = summed[:, :128].astype(BF)
        both = jnp.where(wide == 0, best, summed[:, 128:])
        stat[slot, c] = both.T[:8, :]

        @pl.when(slot != 0)
        def _():
            home = chip(x - slot)
            remote(ob.at[slot, c], oin.at[slot, c], o_send.at[slot, c], o_recv.at[slot, c], home).start()
            remote(stat.at[slot, c], stat_in.at[slot, c], t_send.at[slot, c], t_recv.at[slot, c], home).start()

    def finish(c):
        for d in order:
            remote(ob.at[d, c], oin.at[d, c], o_send.at[d, c], o_recv.at[d, c], chip(x + 1)).wait_recv()
            remote(stat.at[d, c], stat_in.at[d, c], t_send.at[d, c], t_recv.at[d, c], chip(x + 1)).wait_recv()
        stats = [stat[0, c], stat_in[1, c], stat_in[2, c], stat_in[3, c]]
        tops = [s[0:1, :] for s in stats]
        peak = jnp.maximum(jnp.maximum(tops[0], tops[1]), jnp.maximum(tops[2], tops[3]))
        factors = [jnp.exp2(t - peak) for t in tops]
        whole = sum(f * s[1:2, :] for f, s in zip(factors, stats))
        inverse = 1.0 / whole
        row = lax.broadcasted_iota(jnp.int32, (128, rows), 0)
        table = jnp.zeros((128, rows), F32)
        for d in range(4):
            table = jnp.where(row == d, factors[d] * inverse, table)
        columns = table.T
        o = ob[0, c].astype(F32) * columns[:, 0:1]
        for d in range(1, 4):
            o = o + oin[d, c].astype(F32) * columns[:, d : d + 1]
        o = o.astype(BF)
        for head in range(4):
            att[:, head * 128 : (head + 1) * 128] = o[head * tokens : (head + 1) * tokens, :]

    def fill(c, half, d):
        a = wrap(here[half][0] + d)

        def step(b, carry):
            t = b * 4 + a if half == 0 else a * 4 + b
            deep = pl.ds(pl.multiple_of(t * 512, 512), 512)
            r = jnp.dot(att[...], w[deep, half * 256 : (half + 1) * 256], preferred_element_type=F32).astype(BF)
            terms[c, half, a, 0, b] = r[:half_rows]
            terms[c, half, a, 1, b] = r[half_rows:]
            return carry

        lax.fori_loop(0, 4, step, 0, unroll=True)

    def copy(c, half, m, src, dst, partner):
        return remote(src, dst, r_send.at[c, half, m], r_recv.at[c, half, m], partner)

    def moves(c, half):
        def block(d, ch):
            return terms.at[c, half, wrap(here[half][0] + d), ch]

        def block2(d, ch):
            return terms2.at[c, half, ch, wrap(here[half][1] + d)]

        ends = (
            (block(2, 0), relay.at[c, half, 0], first(half, 1)),
            (block(2, 1), relay.at[c, half, 1], first(half, -1)),
            (block(1, 1), inbox.at[c, half, 0, 1], first(half, 1)),
            (block(1, 0), inbox.at[c, half, 0, 0], first(half, 1)),
            (block(-1, 0), inbox.at[c, half, 1, 0], first(half, -1)),
            (block(-1, 1), inbox.at[c, half, 1, 1], first(half, -1)),
            (block2(2, 0), relay2.at[c, half, 0], second(half, 1)),
            (block2(2, 1), relay2.at[c, half, 1], second(half, -1)),
            (block2(1, 1), inbox2.at[c, half, 0, 1], second(half, 1)),
            (block2(1, 0), inbox2.at[c, half, 0, 0], second(half, 1)),
            (block2(-1, 0), inbox2.at[c, half, 1, 0], second(half, -1)),
            (block2(-1, 1), inbox2.at[c, half, 1, 1], second(half, -1)),
        )
        return (lambda m: copy(c, half, m, *ends[m])), ends

    def add(dst, src):
        dst[...] = (dst[...].astype(F32) + src[...].astype(F32)).astype(BF)

    def stage0(c):
        finish(c)
        for half in range(2):
            sends, _ = moves(c, half)
            fill(c, half, 2)
            sends(0).start()
            sends(1).start()
        for half in range(2):
            sends, _ = moves(c, half)
            fill(c, half, 1)
            sends(2).start()
            fill(c, half, -1)
            sends(4).start()
        for half in range(2):
            fill(c, half, 0)

    def stage1(c):
        for half in range(2):
            sends, ends = moves(c, half)
            for m, k in ((0, 3), (1, 5)):
                sends(m).wait_recv()
                add(ends[k][0], ends[m][1])
                sends(k).start()

    def stage2(c):
        for half in range(2):
            sends, _ = moves(c, half)
            for m in (2, 4, 3, 5):
                sends(m).wait_recv()

            def merge(b, carry):
                for ch in range(2):
                    got = terms[c, half, here[half][0], ch, b].astype(F32)
                    got = got + inbox[c, half, 0, ch, b].astype(F32) + inbox[c, half, 1, ch, b].astype(F32)
                    terms2[c, half, ch, b] = got.astype(BF)
                return carry

            lax.fori_loop(0, 4, merge, 0, unroll=True)
            for m in (6, 7, 8, 10):
                sends(m).start()

    def stage3(c):
        for half in range(2):
            sends, ends = moves(c, half)
            for m, k in ((6, 9), (7, 11)):
                sends(m).wait_recv()
                add(ends[k][0], ends[m][1])
                sends(k).start()

    def stage4(c):
        for half in range(2):
            sends, _ = moves(c, half)
            for m in (8, 10, 9, 11):
                sends(m).wait_recv()
            for ch in range(2):
                got = terms2[c, half, ch, here[half][1]].astype(F32)
                got = got + inbox2[c, half, 0, ch].astype(F32) + inbox2[c, half, 1, ch].astype(F32)
                start = c * tokens + ch * half_rows
                out[start : start + half_rows, half * 256 : (half + 1) * 256] = got.astype(BF)

    blocks = 4 * parts
    prepare(0)
    for n in range(4):
        score(0, n, sa, top_a)
    keep.wait()
    remote(fresh, kv.at[:, 1 - core, pl.ds(2048, 256)], swap_send.at[4], swap_recv.at[4], sibling).wait_recv()
    vx[:, 2048:, :128] = kv[1, :, 2048:]
    for n in range(4, 6):
        score(0, n, sa, top_a)

    def half_step(i, now, top_now, later, top_later):
        nxt = jnp.minimum(i + 1, blocks - 1)

        @pl.when(i + 1 < blocks)
        def _():
            prepare(nxt)

        best = jnp.max(top_now[...], axis=1, keepdims=True)
        for n in range(6):
            score(nxt, n, later, top_later)
            weigh(n, now, best)
        settle(i, best)

    def fetched(t, carry):
        fetch(t).wait()
        return carry

    def step(p, carry):
        half_step(2 * p, sa, top_a, sb, top_b)

        @pl.when(p == 2)
        def _():
            lax.fori_loop(0, 16, fetched, 0)
            stage0(0)

        @pl.when(p == 3)
        def _():
            stage1(0)

        half_step(2 * p + 1, sb, top_b, sa, top_a)
        return carry

    lax.fori_loop(0, blocks // 2, step, 0)
    stage2(0)
    stage0(1)
    stage3(0)
    stage1(1)
    stage4(0)
    stage2(1)
    stage3(1)
    stage4(1)
    give.wait_send()
    swaps[0].wait_send()
    swaps[1].wait_send()
    passed.wait_send()
    for c in range(parts):
        for d in order:
            query(c, d).wait_send()
            remote(ob.at[d, c], oin.at[d, c], o_send.at[d, c], o_recv.at[d, c], chip(x + 1)).wait_send()
            remote(stat.at[d, c], stat_in.at[d, c], t_send.at[d, c], t_recv.at[d, c], chip(x + 1)).wait_send()
        for half in range(2):
            sends, _ = moves(c, half)
            for m in range(12):
                sends(m).wait_send()

    def drain(half, m, rows):
        message(half, m, chunk(half, 0, 0), rows, sibling).wait_send()

    for half in range(2):
        drain(half, 0, ALL)
        drain(half, 1, ALL)
        if half == 1:
            drain(half, 2, TOP)
            drain(half, 3, BOTTOM)
        else:
            drain(half, passes, ALL)
        for j in range(4):
            drain(half, 4 + 4 * j, ALL)
            drain(half, 5 + 4 * j, ALL)
            if half == 0:
                drain(half, 6 + 4 * j, TOP)
                drain(half, 7 + 4 * j, BOTTOM)
            else:
                drain(half, 4 + passes + 4 * j, ALL)


def block(hid, gain, wq, wk, wv, cache, w_out, prefix, parts):
    whole = pl.BlockSpec(memory_space=VMEM)
    left = pl.BlockSpec(memory_space=pl.ANY)
    dma = pltpu.SemaphoreType.DMA
    half = np.arange(HEAD_DIM // 2, dtype=np.float64) * 2.0 / HEAD_DIM
    freqs = jnp.asarray(np.tile(500000.0**-half, 2)[None, :], F32)
    rows = 4 * ROWS // parts
    h = rows // 8
    return pl.pallas_call(
        functools.partial(block_kernel, prefix, parts),
        out_shape=jax.ShapeDtypeStruct((ROWS, 512), BF),
        in_specs=[whole] * 3 + [left] * 5,
        out_specs=whole,
        scratch_shapes=[
            pltpu.VMEM((16, CUTS[0][1], 512), BF),
            pltpu.VMEM((16, CUTS[1][1], 512), BF),
            pltpu.VMEM((FEATURES, 512), BF),
            pltpu.VMEM((128, FEATURES), BF),
            pltpu.VMEM((ROWS, 640), F32),
            pltpu.VMEM((ROWS, 128), F32),
            pltpu.VMEM((ROWS, 128), F32),
            pltpu.VMEM((ROWS, 128), F32),
            pltpu.VMEM((ROWS, 128), BF),
            pltpu.VMEM((ROWS, 128), BF),
            pltpu.VMEM((2, ROWS, 128), BF),
            pltpu.VMEM((2, 2, 2304, 128), BF),
            pltpu.VMEM((2, 2304, 256), BF),
            pltpu.VMEM((4, parts, rows, 128), BF),
            pltpu.VMEM((4, parts, rows, 128), BF),
            pltpu.VMEM((4, parts, rows, 128), BF),
            pltpu.VMEM((4, parts, 8, rows), F32),
            pltpu.VMEM((4, parts, 8, rows), F32),
            pltpu.VMEM((rows, 4608), F32),
            pltpu.VMEM((rows, 4608), F32),
            pltpu.VMEM((rows, 128), F32),
            pltpu.VMEM((rows, 128), F32),
            pltpu.VMEM((rows, 256), F32),
            pltpu.VMEM((rows // 4, 512), BF),
            pltpu.VMEM((parts, 2, 4, 2, 4, h, 256), BF),
            pltpu.VMEM((parts, 2, 2, 4, h, 256), BF),
            pltpu.VMEM((parts, 2, 2, 2, 4, h, 256), BF),
            pltpu.VMEM((parts, 2, 2, 4, h, 256), BF),
            pltpu.VMEM((parts, 2, 2, h, 256), BF),
            pltpu.VMEM((parts, 2, 2, 2, h, 256), BF),
            dma((2, 20)),
            dma((2, 20)),
            dma((4,)),
            dma((16,)),
            dma((5,)),
            dma((5,)),
        ]
        + [dma((4, parts))] * 6
        + [dma((parts, 2, 12)), dma((parts, 2, 12))],
        compiler_params=pltpu.CompilerParams(
            collective_id=0, has_side_effects=True, vmem_limit_bytes=62 << 20
        ),
        name="block",
    )(hid, gain, freqs, wq, wk.T, wv.T, cache, w_out)


def body(prefix, parts, hidden_states, norm_gain, w_query, w_key, w_value, cache, w_out):
    gain = norm_gain.reshape(1, FEATURES)
    return block(hidden_states, gain, w_query, w_key, w_value, cache, w_out, prefix, parts)


def solution(mesh):
    in_specs = (P("grp", "tp"), P(), P(None, "tp"), P(None, "tp"), P(None, "tp"), P("grp", "tp"), P("tp", None))
    return jax.shard_map(
        functools.partial(body, 16384, 2),
        mesh=mesh,
        in_specs=in_specs,
        out_specs=P("grp", "tp"),
        check_vma=False,
    )
```

```python
import functools
import math

import jax
import jax.numpy as jnp
import numpy as np
from jax import lax
from jax.experimental import pallas as pl
from jax.experimental.pallas import tpu as pltpu
from jax.sharding import PartitionSpec as P

HEAD_DIM = 128
MESH = pl.DeviceIdType.MESH
BF = jnp.bfloat16
F32 = jnp.float32
ROWS = 256
FEATURES = 8192
CUTS = ((0, 160), (160, 96))
PIECES = ((0, 0, 1024), (0, 1024, 1024), (1, 0, 1024), (1, 1024, 1024), (0, 2048, 256), (1, 2048, 256))
NEG = -1e30
VMEM = pltpu.MemorySpace.VMEM


def place():
    grp = lax.axis_index("grp")
    tp = lax.axis_index("tp")
    return grp // 2, grp % 2, tp // 4, tp % 4


def wrap(i):
    return lax.rem(i + 8, 4)


def greet(partners):
    barrier = pltpu.get_barrier_semaphore()
    for partner in partners:
        pl.semaphore_signal(barrier, inc=1, device_id=partner, device_id_type=MESH)
    pl.semaphore_wait(barrier, len(partners))


def remote(src, dst, send, recv, partner):
    return pltpu.make_async_remote_copy(
        src_ref=src, dst_ref=dst, send_sem=send, recv_sem=recv, device_id=partner, device_id_type=MESH
    )


def block_kernel(
    prefix, parts, hid, gain, freqs, wq_hbm, wk_hbm, wv_hbm, cache, w_hbm,
    out,
    got_a, got_b, w, wkv, acc, squares, cos, sin, part, partner_part, fresh, kv, vx,
    qs, ob, oin, stat, stat_in, sa, sb, top_a, top_b, summed, att,
    terms, relay, inbox, terms2, relay2, inbox2,
    send, recv, load, w_load, swap_send, swap_recv,
    q_send, q_recv, o_send, o_recv, t_send, t_recv, r_send, r_recv,
):
    got = (got_a, got_b)
    tokens = ROWS // parts
    rows = 4 * tokens
    half_rows = tokens // 2
    x, core, z, y = place()
    grp = 2 * x + core
    parity = lax.rem(y, 2)

    def at(dz, dy):
        return wrap(z + dz) * 4 + wrap(y + dy)

    def to(dz, dy):
        return {"grp": grp, "tp": at(dz, dy)}

    def chip(i):
        return {"grp": 2 * wrap(i) + core, "tp": z * 4 + y}

    def chunk(half, a, b):
        return at(b, a) if half == 0 else at(a, b)

    def first(half, d):
        return to(0, d) if half == 0 else to(d, 0)

    def second(half, d):
        return to(d, 0) if half == 0 else to(0, d)

    partner = {"grp": grp, "tp": z * 4 + y + 1 - 2 * parity}
    sibling = {"grp": grp + 1 - 2 * core, "tp": z * 4 + y}
    loads = [
        pltpu.make_async_copy(wq_hbm, w, load.at[0]),
        pltpu.make_async_copy(wk_hbm, wkv.at[pl.ds(0, 64)], load.at[1]),
        pltpu.make_async_copy(wv_hbm, wkv.at[pl.ds(64, 64)], load.at[2]),
    ]
    for one in loads:
        one.start()
    own_cache = pltpu.make_async_copy(cache, kv.at[parity, core, pl.ds(0, 2048)], load.at[3])
    own_cache.start()
    for half, (start, size) in enumerate(CUTS):
        got[half][at(0, 0)] = hid[start : start + size, :]
    order = (3, 2, 1)
    greet([to(0, 1), to(0, -1), to(1, 0), to(-1, 0), sibling, chip(x + 1), chip(x + 2), chip(x + 3)])

    TOP, BOTTOM, ALL = 0, 1, 2
    on = jnp.where(parity == 0, -1, 1)
    passes, takes = 3 - parity, 2 + parity

    def message(half, m, idx, which, partner):
        size = CUTS[half][1]
        ref = got[half].at[idx, pl.ds(which % 2 * size // 2, size if which == ALL else size // 2)]
        return remote(ref, ref, send.at[half, m], recv.at[half, m], partner)

    for m, d in ((0, 1), (1, -1)):
        for half in range(2):
            message(half, m, chunk(half, 0, 0), ALL, first(half, d)).start()
    for m, d in ((4, 1), (5, -1)):
        for half in range(2):
            message(half, m, chunk(half, 0, 0), ALL, second(half, d)).start()
    mine = kv.at[parity, core, pl.ds(0, 2048)]
    swaps = [
        remote(cache, mine, swap_send.at[0], swap_recv.at[0], partner),
        remote(cache, mine, swap_send.at[1], swap_recv.at[1], sibling),
    ]
    for one in swaps:
        one.start()
    acc[...] = jnp.zeros_like(acc)
    vx[:, :, 128:] = jnp.ones((2, 2304, 128), BF)
    squares[...] = jnp.zeros_like(squares)

    def absorb(half, t):
        start, size = CUTS[half]
        here = slice(start, start + size)
        h = got[half][t].astype(F32)
        sq = h * h
        squares[here] += sq[:, :128] + sq[:, 128:256] + sq[:, 256:384] + sq[:, 384:]
        depth = pl.ds(pl.multiple_of(t * 512, 512), 512)
        scaled = (h * gain[:, depth]).astype(BF)
        acc[here, :512] += jnp.dot(scaled, w[depth, :], preferred_element_type=F32)
        acc[here, 512:] += lax.dot_general(
            scaled, wkv[:, depth], (((1,), (1,)), ((), ())), preferred_element_type=F32
        )

    def absorb_all(count, place_of):
        def step(i, carry):
            for half in range(2):
                absorb(half, chunk(half, *place_of(i)))
            return carry

        lax.fori_loop(0, count, step, 0)

    def arrived(half, m, idx, rows):
        message(half, m, idx, rows, sibling).wait_recv()

    def spread(half, j, idx):
        message(half, 4 + 4 * j, idx, ALL, second(half, 1)).start()
        message(half, 5 + 4 * j, idx, ALL, second(half, -1)).start()

    lane = lax.broadcasted_iota(jnp.int32, (ROWS, 128), 1)
    row = lax.broadcasted_iota(jnp.int32, (ROWS, 128), 0)
    angles = (row + (prefix + grp * ROWS)).astype(F32) * freqs[...]
    cos[...] = jnp.cos(angles)
    sine = jnp.sin(angles)
    sin[...] = jnp.where(lane < 64, -sine, sine)
    for one in loads:
        one.wait()
    absorb_all(1, lambda i: (0, 0))
    for half in range(2):
        idx = chunk(half, -1, 0)
        arrived(half, 0, idx, ALL)
        if half == 1:
            message(half, 2, idx, TOP, first(half, 1)).start()
        spread(half, 1, idx)
    for half in range(2):
        idx = chunk(half, 1, 0)
        arrived(half, 1, idx, ALL)
        if half == 1:
            message(half, 3, idx, BOTTOM, first(half, -1)).start()
        else:
            message(half, passes, chunk(half, -on, 0), ALL, first(half, on)).start()
        spread(half, 2, idx)
    absorb_all(2, lambda i: (2 * i - 1, 0))

    def neighbours(j, a):
        for half in range(2):
            idx = chunk(half, a, -1)
            arrived(half, 4 + 4 * j, idx, ALL)
            if half == 0:
                message(half, 6 + 4 * j, idx, TOP, second(half, 1)).start()
            idx = chunk(half, a, 1)
            arrived(half, 5 + 4 * j, idx, ALL)
            if half == 0:
                message(half, 7 + 4 * j, idx, BOTTOM, second(half, -1)).start()
            else:
                message(half, 4 + passes + 4 * j, chunk(half, a, -on), ALL, second(half, on)).start()
        absorb_all(2, lambda i: (a, 2 * i - 1))

    def opposite(j, a):
        for half in range(2):
            idx = chunk(half, a, 2)
            if half == 0:
                arrived(half, 6 + 4 * j, idx, TOP)
                arrived(half, 7 + 4 * j, idx, BOTTOM)
            else:
                arrived(half, 4 + takes + 4 * j, idx, ALL)
        absorb_all(1, lambda i: (a, 2))

    neighbours(0, 0)
    for half in range(2):
        idx = chunk(half, 2, 0)
        if half == 1:
            arrived(half, 2, idx, TOP)
            arrived(half, 3, idx, BOTTOM)
        else:
            arrived(half, takes, idx, ALL)
        spread(half, 3, idx)
    absorb_all(1, lambda i: (2, 0))

    def sweep(j, carry):
        neighbours(j, jnp.where(j == 1, -1, j - 1))
        return carry

    lax.fori_loop(1, 4, sweep, 0)
    theirs = kv.at[1 - parity, core, pl.ds(0, 2048)]
    remote(cache, theirs, swap_send.at[0], swap_recv.at[0], partner).wait_recv()
    passed = remote(theirs, theirs, swap_send.at[2], swap_recv.at[2], sibling)
    passed.start()

    def sweep_far(j, carry):
        opposite(j, jnp.where(j == 0, 0, jnp.where(j == 1, -1, j - 1)))
        return carry

    lax.fori_loop(0, 4, sweep_far, 0)

    mean = jnp.sum(squares[...], axis=1, keepdims=True) * (1.0 / FEATURES)
    root = lax.rsqrt(mean + 1e-05)
    own = acc[:, 512:] * root
    part[...] = own.astype(BF)
    swap = remote(part, partner_part, swap_send.at[3], swap_recv.at[3], partner)
    swap.start()
    def rope(v):
        return v * cos[...] + pltpu.roll(v, 64, 1) * sin[...]

    scale = math.log2(math.e) / math.sqrt(HEAD_DIM)
    for head in range(4):
        turned = (rope(acc[:, head * 128 : (head + 1) * 128] * root) * scale).astype(BF)
        for i in range(parts):
            qs[0, i, head * tokens : (head + 1) * tokens, :] = turned[i * tokens : (i + 1) * tokens, :]

    def query(c, d):
        return remote(qs.at[0, c], qs.at[d, c], q_send.at[d, c], q_recv.at[d, c], chip(x + d))

    for c in range(parts):
        for d in order:
            query(c, d).start()

    def fetch(t):
        spot = w.at[pl.ds(pl.multiple_of(t * 512, 512), 512)]
        return pltpu.make_async_copy(w_hbm.at[:, pl.ds(pl.multiple_of(t * 512, 512), 512)], spot, w_load.at[t])

    def begin(t, carry):
        fetch(t).start()
        return carry

    lax.fori_loop(0, 16, begin, 0)
    swap.wait()
    other = partner_part[...].astype(F32)
    left = jnp.where(parity == 0, own, other)
    right = jnp.where(parity == 0, other, own)
    key = jnp.where(lane < 64, left, pltpu.roll(right, 64, 1))
    value = jnp.where(lane < 64, pltpu.roll(left, 64, 1), right)
    fresh[0] = rope(key).astype(BF)
    fresh[1] = value.astype(BF)
    spot = kv.at[:, core, pl.ds(2048, 256)]
    keep = pltpu.make_async_copy(fresh, spot, load.at[0])
    keep.start()
    give = remote(fresh, spot, swap_send.at[4], swap_recv.at[4], sibling)
    give.start()
    own_cache.wait()
    remote(cache, kv.at[parity, 1 - core, pl.ds(0, 2048)], swap_send.at[1], swap_recv.at[1], sibling).wait_recv()
    remote(
        cache, kv.at[1 - parity, 1 - core, pl.ds(0, 2048)], swap_send.at[2], swap_recv.at[2], sibling
    ).wait_recv()
    vx[:, :2048, :128] = kv[1, :, :2048]
    here = ((y, z), (z, y))
    diff = lax.broadcasted_iota(jnp.int32, (rows, 256), 1) - lax.rem(
        lax.broadcasted_iota(jnp.int32, (rows, 256), 0), tokens
    )

    def block_of(i):
        c, k = i // 4, lax.rem(i, 4)
        k = jnp.where(c == 0, k, lax.rem(k + 1, 4))
        return c, jnp.where(k == 0, 0, 4 - k)

    def prepare(i):
        c, slot = block_of(i)

        @pl.when(slot != 0)
        def _():
            remote(qs.at[0, 0], qs.at[slot, c], q_send.at[slot, c], q_recv.at[slot, c], chip(x + 1)).wait_recv()

    def score(i, n, s_ref, top_ref):
        c, slot = block_of(i)
        b, start, size = PIECES[n]
        s = lax.dot_general(
            qs[slot, c], kv[0, b, start : start + size, :], (((1,), (1,)), ((), ())), preferred_element_type=F32
        )
        if size == 256:
            ahead = (2 * wrap(x - slot) + core - 2 * x - b) * ROWS + c * tokens
            s = jnp.where(diff <= ahead, s, NEG)
        s_ref[:, b * 2304 + start : b * 2304 + start + size] = s
        top = s[:, :128]
        for k in range(1, size // 128):
            top = jnp.maximum(top, s[:, k * 128 : (k + 1) * 128])
        top_ref[...] = top if n == 0 else jnp.maximum(top_ref[...], top)

    def weigh(n, s_ref, best):
        b, start, size = PIECES[n]
        p = jnp.exp2(s_ref[:, b * 2304 + start : b * 2304 + start + size] - best)
        o = jnp.dot(p.astype(BF), vx[b, start : start + size, :], preferred_element_type=F32)
        summed[...] = o if n == 0 else summed[...] + o

    wide = lax.broadcasted_iota(jnp.int32, (rows, 128), 1)

    def settle(i, best):
        c, slot = block_of(i)
        ob[slot, c] = summed[:, :128].astype(BF)
        both = jnp.where(wide == 0, best, summed[:, 128:])
        stat[slot, c] = both.T[:8, :]

        @pl.when(slot != 0)
        def _():
            home = chip(x - slot)
            remote(ob.at[slot, c], oin.at[slot, c], o_send.at[slot, c], o_recv.at[slot, c], home).start()
            remote(stat.at[slot, c], stat_in.at[slot, c], t_send.at[slot, c], t_recv.at[slot, c], home).start()

    def finish(c):
        for d in order:
            remote(ob.at[d, c], oin.at[d, c], o_send.at[d, c], o_recv.at[d, c], chip(x + 1)).wait_recv()
            remote(stat.at[d, c], stat_in.at[d, c], t_send.at[d, c], t_recv.at[d, c], chip(x + 1)).wait_recv()
        stats = [stat[0, c], stat_in[1, c], stat_in[2, c], stat_in[3, c]]
        tops = [s[0:1, :] for s in stats]
        peak = jnp.maximum(jnp.maximum(tops[0], tops[1]), jnp.maximum(tops[2], tops[3]))
        factors = [jnp.exp2(t - peak) for t in tops]
        whole = sum(f * s[1:2, :] for f, s in zip(factors, stats))
        inverse = 1.0 / whole
        row = lax.broadcasted_iota(jnp.int32, (128, rows), 0)
        table = jnp.zeros((128, rows), F32)
        for d in range(4):
            table = jnp.where(row == d, factors[d] * inverse, table)
        columns = table.T
        o = ob[0, c].astype(F32) * columns[:, 0:1]
        for d in range(1, 4):
            o = o + oin[d, c].astype(F32) * columns[:, d : d + 1]
        o = o.astype(BF)
        for head in range(4):
            att[:, head * 128 : (head + 1) * 128] = o[head * tokens : (head + 1) * tokens, :]

    def fill(c, half, d):
        a = wrap(here[half][0] + d)

        def step(b, carry):
            t = b * 4 + a if half == 0 else a * 4 + b
            deep = pl.ds(pl.multiple_of(t * 512, 512), 512)
            r = jnp.dot(att[...], w[deep, half * 256 : (half + 1) * 256], preferred_element_type=F32).astype(BF)
            terms[c, half, a, 0, b] = r[:half_rows]
            terms[c, half, a, 1, b] = r[half_rows:]
            return carry

        lax.fori_loop(0, 4, step, 0, unroll=True)

    def copy(c, half, m, src, dst, partner):
        return remote(src, dst, r_send.at[c, half, m], r_recv.at[c, half, m], partner)

    def moves(c, half):
        def block(d, ch):
            return terms.at[c, half, wrap(here[half][0] + d), ch]

        def block2(d, ch):
            return terms2.at[c, half, ch, wrap(here[half][1] + d)]

        ends = (
            (block(2, 0), relay.at[c, half, 0], first(half, 1)),
            (block(2, 1), relay.at[c, half, 1], first(half, -1)),
            (block(1, 1), inbox.at[c, half, 0, 1], first(half, 1)),
            (block(1, 0), inbox.at[c, half, 0, 0], first(half, 1)),
            (block(-1, 0), inbox.at[c, half, 1, 0], first(half, -1)),
            (block(-1, 1), inbox.at[c, half, 1, 1], first(half, -1)),
            (block2(2, 0), relay2.at[c, half, 0], second(half, 1)),
            (block2(2, 1), relay2.at[c, half, 1], second(half, -1)),
            (block2(1, 1), inbox2.at[c, half, 0, 1], second(half, 1)),
            (block2(1, 0), inbox2.at[c, half, 0, 0], second(half, 1)),
            (block2(-1, 0), inbox2.at[c, half, 1, 0], second(half, -1)),
            (block2(-1, 1), inbox2.at[c, half, 1, 1], second(half, -1)),
        )
        return (lambda m: copy(c, half, m, *ends[m])), ends

    def add(dst, src):
        dst[...] = (dst[...].astype(F32) + src[...].astype(F32)).astype(BF)

    def stage0(c):
        finish(c)
        for half in range(2):
            sends, _ = moves(c, half)
            fill(c, half, 2)
            sends(0).start()
            sends(1).start()
        for half in range(2):
            sends, _ = moves(c, half)
            fill(c, half, 1)
            sends(2).start()
            fill(c, half, -1)
            sends(4).start()
        for half in range(2):
            fill(c, half, 0)

    def stage1(c):
        for half in range(2):
            sends, ends = moves(c, half)
            for m, k in ((0, 3), (1, 5)):
                sends(m).wait_recv()
                add(ends[k][0], ends[m][1])
                sends(k).start()

    def stage2(c):
        for half in range(2):
            sends, _ = moves(c, half)
            for m in (2, 4, 3, 5):
                sends(m).wait_recv()

            def merge(b, carry):
                for ch in range(2):
                    got = terms[c, half, here[half][0], ch, b].astype(F32)
                    got = got + inbox[c, half, 0, ch, b].astype(F32) + inbox[c, half, 1, ch, b].astype(F32)
                    terms2[c, half, ch, b] = got.astype(BF)
                return carry

            lax.fori_loop(0, 4, merge, 0, unroll=True)
            for m in (6, 7, 8, 10):
                sends(m).start()

    def stage3(c):
        for half in range(2):
            sends, ends = moves(c, half)
            for m, k in ((6, 9), (7, 11)):
                sends(m).wait_recv()
                add(ends[k][0], ends[m][1])
                sends(k).start()

    def stage4(c):
        for half in range(2):
            sends, _ = moves(c, half)
            for m in (8, 10, 9, 11):
                sends(m).wait_recv()
            for ch in range(2):
                got = terms2[c, half, ch, here[half][1]].astype(F32)
                got = got + inbox2[c, half, 0, ch].astype(F32) + inbox2[c, half, 1, ch].astype(F32)
                start = c * tokens + ch * half_rows
                out[start : start + half_rows, half * 256 : (half + 1) * 256] = got.astype(BF)

    blocks = 4 * parts
    prepare(0)
    for n in range(4):
        score(0, n, sa, top_a)
    keep.wait()
    remote(fresh, kv.at[:, 1 - core, pl.ds(2048, 256)], swap_send.at[4], swap_recv.at[4], sibling).wait_recv()
    vx[:, 2048:, :128] = kv[1, :, 2048:]
    for n in range(4, 6):
        score(0, n, sa, top_a)

    def half_step(i, now, top_now, later, top_later):
        nxt = jnp.minimum(i + 1, blocks - 1)

        @pl.when(i + 1 < blocks)
        def _():
            prepare(nxt)

        best = jnp.max(top_now[...], axis=1, keepdims=True)
        for n in range(6):
            score(nxt, n, later, top_later)
            weigh(n, now, best)
        settle(i, best)

    def fetched(t, carry):
        fetch(t).wait()
        return carry

    def step(p, carry):
        half_step(2 * p, sa, top_a, sb, top_b)

        @pl.when(p == 2)
        def _():
            lax.fori_loop(0, 16, fetched, 0)
            stage0(0)

        @pl.when(p == 3)
        def _():
            stage1(0)

        half_step(2 * p + 1, sb, top_b, sa, top_a)
        return carry

    lax.fori_loop(0, blocks // 2, step, 0)
    stage2(0)
    stage0(1)
    stage3(0)
    stage1(1)
    stage4(0)
    stage2(1)
    stage3(1)
    stage4(1)
    give.wait_send()
    swaps[0].wait_send()
    swaps[1].wait_send()
    passed.wait_send()
    for c in range(parts):
        for d in order:
            query(c, d).wait_send()
            remote(ob.at[d, c], oin.at[d, c], o_send.at[d, c], o_recv.at[d, c], chip(x + 1)).wait_send()
            remote(stat.at[d, c], stat_in.at[d, c], t_send.at[d, c], t_recv.at[d, c], chip(x + 1)).wait_send()
        for half in range(2):
            sends, _ = moves(c, half)
            for m in range(12):
                sends(m).wait_send()

    def drain(half, m, rows):
        message(half, m, chunk(half, 0, 0), rows, sibling).wait_send()

    for half in range(2):
        drain(half, 0, ALL)
        drain(half, 1, ALL)
        if half == 1:
            drain(half, 2, TOP)
            drain(half, 3, BOTTOM)
        else:
            drain(half, passes, ALL)
        for j in range(4):
            drain(half, 4 + 4 * j, ALL)
            drain(half, 5 + 4 * j, ALL)
            if half == 0:
                drain(half, 6 + 4 * j, TOP)
                drain(half, 7 + 4 * j, BOTTOM)
            else:
                drain(half, 4 + passes + 4 * j, ALL)


def block(hid, gain, wq, wk, wv, cache, w_out, prefix, parts):
    whole = pl.BlockSpec(memory_space=VMEM)
    left = pl.BlockSpec(memory_space=pl.ANY)
    dma = pltpu.SemaphoreType.DMA
    half = np.arange(HEAD_DIM // 2, dtype=np.float64) * 2.0 / HEAD_DIM
    freqs = jnp.asarray(np.tile(500000.0**-half, 2)[None, :], F32)
    rows = 4 * ROWS // parts
    h = rows // 8
    return pl.pallas_call(
        functools.partial(block_kernel, prefix, parts),
        out_shape=jax.ShapeDtypeStruct((ROWS, 512), BF),
        in_specs=[whole] * 3 + [left] * 5,
        out_specs=whole,
        scratch_shapes=[
            pltpu.VMEM((16, CUTS[0][1], 512), BF),
            pltpu.VMEM((16, CUTS[1][1], 512), BF),
            pltpu.VMEM((FEATURES, 512), BF),
            pltpu.VMEM((128, FEATURES), BF),
            pltpu.VMEM((ROWS, 640), F32),
            pltpu.VMEM((ROWS, 128), F32),
            pltpu.VMEM((ROWS, 128), F32),
            pltpu.VMEM((ROWS, 128), F32),
            pltpu.VMEM((ROWS, 128), BF),
            pltpu.VMEM((ROWS, 128), BF),
            pltpu.VMEM((2, ROWS, 128), BF),
            pltpu.VMEM((2, 2, 2304, 128), BF),
            pltpu.VMEM((2, 2304, 256), BF),
            pltpu.VMEM((4, parts, rows, 128), BF),
            pltpu.VMEM((4, parts, rows, 128), BF),
            pltpu.VMEM((4, parts, rows, 128), BF),
            pltpu.VMEM((4, parts, 8, rows), F32),
            pltpu.VMEM((4, parts, 8, rows), F32),
            pltpu.VMEM((rows, 4608), F32),
            pltpu.VMEM((rows, 4608), F32),
            pltpu.VMEM((rows, 128), F32),
            pltpu.VMEM((rows, 128), F32),
            pltpu.VMEM((rows, 256), F32),
            pltpu.VMEM((rows // 4, 512), BF),
            pltpu.VMEM((parts, 2, 4, 2, 4, h, 256), BF),
            pltpu.VMEM((parts, 2, 2, 4, h, 256), BF),
            pltpu.VMEM((parts, 2, 2, 2, 4, h, 256), BF),
            pltpu.VMEM((parts, 2, 2, 4, h, 256), BF),
            pltpu.VMEM((parts, 2, 2, h, 256), BF),
            pltpu.VMEM((parts, 2, 2, 2, h, 256), BF),
            dma((2, 20)),
            dma((2, 20)),
            dma((4,)),
            dma((16,)),
            dma((5,)),
            dma((5,)),
        ]
        + [dma((4, parts))] * 6
        + [dma((parts, 2, 12)), dma((parts, 2, 12))],
        compiler_params=pltpu.CompilerParams(
            collective_id=0, has_side_effects=True, vmem_limit_bytes=62 << 20
        ),
        name="block",
    )(hid, gain, freqs, wq, wk.T, wv.T, cache, w_out)


def body(prefix, parts, hidden_states, norm_gain, w_query, w_key, w_value, cache, w_out):
    gain = norm_gain.reshape(1, FEATURES)
    return block(hidden_states, gain, w_query, w_key, w_value, cache, w_out, prefix, parts)


def solution(mesh):
    in_specs = (P("grp", "tp"), P(), P(None, "tp"), P(None, "tp"), P(None, "tp"), P("grp", "tp"), P("tp", None))
    return jax.shard_map(
        functools.partial(body, 16384, 2),
        mesh=mesh,
        in_specs=in_specs,
        out_specs=P("grp", "tp"),
        check_vma=False,
    )
```
